32 devices in a mesh: mp: 2 (over x), proj: 16 (over z, y, core).
Axes of the slice: x: 2, y: 2, z: 4, core: 2. Of those that a mesh axis runs over, the one named last changes fastest.
Arguments:
- normed_hidden_input: bfloat16 [2048, 5120], P('proj', 'mp'), may hold values from -6 to 6
- attention_mixture: bfloat16 [2048, 5120], P('proj', 'mp'), may hold values from -6 to 6
- normed_gate_input: bfloat16 [2048, 5120], P('proj', 'mp'), may hold values from -6 to 6
- down_projection_input: bfloat16 [2048, 27648], P('proj', 'mp'), may hold values from -6 to 6
- query_out_cotangent: bfloat16 [2048, 5120], P('proj', 'mp'), may hold values from -6 to 6
- key_value_cotangents: bfloat16 [2048, 2, 1024], P('proj', None, 'mp'), may hold values from -6 to 6
- attention_out_cotangent: bfloat16 [2048, 5120], P('proj', 'mp'), may hold values from -6 to 6
- gate_up_cotangents: bfloat16 [2048, 2, 27648], P('proj', None, 'mp'), may hold values from -6 to 6
- down_out_cotangent: bfloat16 [2048, 5120], P('proj', 'mp'), may hold values from -6 to 6
- adapter_input_factors: bfloat16 [6, 8, 5120], P(None, None, 'mp'), may hold values from -0.078125 to 0.078125
- down_adapter_input_factor: bfloat16 [8, 27648], P(None, 'mp'), may hold values from -0.0390625 to 0.0390625
- adapter_output_factors: bfloat16 [3, 8, 5120], P(None, None, 'mp'), may hold values from -0.078125 to 0.078125
- key_value_adapter_output: bfloat16 [2, 8, 1024], P(None, None, 'mp'), may hold values from -0.1875 to 0.1875
- gate_up_adapter_output: bfloat16 [2, 8, 27648], P(None, None, 'mp'), may hold values from -0.0390625 to 0.0390625
- verified_loss_mask: int32 [2048], P('proj'), may hold values 0 or 1
- block_projector_seeds: int32 [14], replicated, may hold values from 0 to 16777215
Outputs:
- features: float32 [1, 2048], P(None, ('mp', 'proj'))
The draws below stay inside these ranges and needn't reach their ends.
All inputs are finite; a program needn't handle non-finite values. No bound on the sum of `verified_loss_mask` on one device may be relied on, other than what follows from the above.
Results may differ from the reference program's by a relative error of at most 0.0028.
Values sent between devices are 32-bit elements; how exact they have to be, the bound alone decides.
No kernel may reach another device: no remote copies, remote signals or barrier semaphores. Data moves between devices by JAX's collectives and lax.ppermute only.
A program may use at most 64 MiB of HBM per device.

```python
import math
import jax
import jax.numpy as jnp
from jax import lax

MODEL_WIDTH = 5120
FEEDFORWARD_UNITS = 27648
KEY_WIDTH = 1024
ADAPTER_RANK = 8
K = 2048
LENGTH = 2048
SEGS = 14
TOKENS = 2048
EXAMPLES = 1


def touch_ends(result, key, low, largest):
    spot = [jax.random.randint(jax.random.fold_in(key, axis), (), 0, length) for axis, length in enumerate(result.shape)]
    main_axis = result.shape.index(max(result.shape))
    neighbour = spot[:main_axis] + [(spot[main_axis] + 1) % result.shape[main_axis]] + spot[main_axis + 1:]
    return result.at[tuple(spot)].set(low).at[tuple(neighbour)].set(largest)


def steps_of(rng, shape, pieces, least, top_value):
    loudness = 1.0
    for dim, shards_of in pieces:
        steps = jax.random.uniform(jax.random.fold_in(jax.random.fold_in(rng, 6), dim), (shards_of,), jnp.float32, least / len(pieces), top_value / len(pieces))
        loudness = loudness * jnp.repeat(jnp.exp(steps), shape[dim] // shards_of).reshape((-1,) + (1,) * (len(shape) - 1 - dim))
    return loudness


def gaussian(own_key, extent, width, reach, shards=(), kind=jnp.bfloat16):
    values = jax.random.normal(own_key, extent, jnp.float32) * width
    if len(shards) > 0:
        values = steps_of(own_key, extent, shards, -0.22, 0.18) * values
    return jnp.clip(values, min=-reach, max=reach).astype(kind)


def setup_inputs(seed: int = 0) -> dict:
    splits = jax.random.split(jax.random.key(seed), 17)
    normed_hidden_input = gaussian(splits[0], (TOKENS, MODEL_WIDTH), 1.0, 6.0, ((0, 16), (1, 2)))
    attention_mixture = gaussian(splits[1], (TOKENS, MODEL_WIDTH), 1.0, 6.0, ((0, 16), (1, 2)))
    normed_gate_input = gaussian(splits[2], (TOKENS, MODEL_WIDTH), 1.0, 6.0, ((0, 16), (1, 2)))
    down_projection_input = gaussian(splits[3], (TOKENS, FEEDFORWARD_UNITS), 1.0, 6.0, ((0, 16), (1, 2)))
    query_out_cotangent = gaussian(splits[4], (TOKENS, MODEL_WIDTH), 1.0, 6.0, ((0, 16), (1, 2)))
    key_value_cotangents = gaussian(splits[5], (TOKENS, 2, KEY_WIDTH), 1.0, 6.0, ((0, 16), (2, 2)))
    attention_out_cotangent = gaussian(splits[6], (TOKENS, MODEL_WIDTH), 1.0, 6.0, ((0, 16), (1, 2)))
    gate_up_cotangents = gaussian(splits[7], (TOKENS, 2, FEEDFORWARD_UNITS), 1.0, 6.0, ((0, 16), (2, 2)))
    down_out_cotangent = gaussian(splits[8], (TOKENS, MODEL_WIDTH), 1.0, 6.0, ((0, 16), (1, 2)))
    adapter_input_factors = gaussian(splits[9], (6, ADAPTER_RANK, MODEL_WIDTH), MODEL_WIDTH ** -0.5, 0.078125, ((2, 2),))
    down_adapter_input_factor = gaussian(splits[10], (ADAPTER_RANK, FEEDFORWARD_UNITS), FEEDFORWARD_UNITS ** -0.5, 0.0390625, ((1, 2),))
    adapter_output_factors = gaussian(splits[11], (3, ADAPTER_RANK, MODEL_WIDTH), MODEL_WIDTH ** -0.5, 0.078125, ((2, 2),))
    key_value_adapter_output = gaussian(splits[12], (2, ADAPTER_RANK, KEY_WIDTH), KEY_WIDTH ** -0.5, 0.1875, ((2, 2),))
    gate_up_adapter_output = gaussian(splits[13], (2, ADAPTER_RANK, FEEDFORWARD_UNITS), FEEDFORWARD_UNITS ** -0.5, 0.0390625, ((2, 2),))
    verified_loss_mask = touch_ends((jax.random.randint(splits[14], (TOKENS,), 0, 4) < 3).astype(jnp.int32), jax.random.fold_in(splits[14], 1), 0, 1)
    block_projector_seeds = touch_ends(jax.random.randint(splits[15], (SEGS,), 0, 16777216), jax.random.fold_in(splits[15], 1), 0, 16777215).astype(jnp.int32)
    return dict(normed_hidden_input=normed_hidden_input, attention_mixture=attention_mixture, normed_gate_input=normed_gate_input, down_projection_input=down_projection_input, query_out_cotangent=query_out_cotangent, key_value_cotangents=key_value_cotangents, attention_out_cotangent=attention_out_cotangent, gate_up_cotangents=gate_up_cotangents, down_out_cotangent=down_out_cotangent, adapter_input_factors=adapter_input_factors, down_adapter_input_factor=down_adapter_input_factor, adapter_output_factors=adapter_output_factors, key_value_adapter_output=key_value_adapter_output, gate_up_adapter_output=gate_up_adapter_output, verified_loss_mask=verified_loss_mask, block_projector_seeds=block_projector_seeds)


def mix_bits(row_keys, col_keys):
    hashed = row_keys[:, None] ^ col_keys[None, :]
    hashed = hashed ^ hashed >> 16 & 65535
    hashed = hashed * -2048144789
    hashed = hashed ^ hashed >> 13 & 524287
    hashed = hashed * -1028477387
    hashed = hashed ^ hashed >> 16 & 65535
    byte_sum = (hashed & 255) + (hashed >> 8 & 255) + (hashed >> 16 & 255) + (hashed >> 24 & 255)
    return (byte_sum - 510).astype(jnp.float32)

def project_rows(gradients, row_keys, col_keys, block_limit):
    row_count = gradients.shape[1]
    block_rows = math.gcd(row_count, block_limit)

    def add_block(number, accumulated):
        first_row = (number * block_rows).astype(jnp.int32)
        grad_block = lax.dynamic_slice_in_dim(gradients, first_row, block_rows, 1)
        key_block = lax.dynamic_slice_in_dim(row_keys, first_row, block_rows, 0)
        table = mix_bits(key_block, col_keys)
        return accumulated + jnp.dot(grad_block, table, precision=lax.Precision.HIGHEST, preferred_element_type=jnp.float32)
    zero_acc = jnp.zeros((gradients.shape[0], col_keys.shape[0]), jnp.float32)
    return lax.fori_loop(0, row_count // block_rows, add_block, zero_acc)

def segment_keys(seg_width, seed_value):
    positions = jnp.arange(ADAPTER_RANK * seg_width, dtype=jnp.int32)
    rank_pos = positions // seg_width
    feature = positions % seg_width
    return seed_value * 1103515245 + (feature * ADAPTER_RANK + rank_pos) * 668265263

def example_grads(inputs, cotangent, factor_a, factor_b, weights):
    act_a = jnp.dot(inputs, factor_a.T, preferred_element_type=jnp.float32)
    act_b = jnp.dot(cotangent, factor_b.T, preferred_element_type=jnp.float32)
    masked_v = (weights * act_a).astype(jnp.bfloat16)
    masked_u = (weights * act_b).astype(jnp.bfloat16)
    in_width = inputs.shape[1]
    out_width = cotangent.shape[1]

    def one_rollout(packed):
        rollout_in, rollout_cot, rollout_u, rollout_v = packed
        grad_a = jnp.dot(rollout_u.T, rollout_in, preferred_element_type=jnp.float32)
        grad_b = jnp.dot(rollout_v.T, rollout_cot, preferred_element_type=jnp.float32)
        return (grad_a.reshape(-1), grad_b.reshape(-1))
    return lax.map(one_rollout, (inputs.reshape(EXAMPLES, LENGTH, in_width), cotangent.reshape(EXAMPLES, LENGTH, out_width), masked_u.reshape(EXAMPLES, LENGTH, ADAPTER_RANK), masked_v.reshape(EXAMPLES, LENGTH, ADAPTER_RANK)))

def reference(normed_hidden_input, attention_mixture, normed_gate_input, down_projection_input, query_out_cotangent, key_value_cotangents, attention_out_cotangent, gate_up_cotangents, down_out_cotangent, adapter_input_factors, down_adapter_input_factor, adapter_output_factors, key_value_adapter_output, gate_up_adapter_output, verified_loss_mask, block_projector_seeds):
    weights = verified_loss_mask.astype(jnp.float32)[:, None]
    block_triplets = [(normed_hidden_input, query_out_cotangent, adapter_input_factors[0], adapter_output_factors[0]), (normed_hidden_input, key_value_cotangents[:, 0], adapter_input_factors[1], key_value_adapter_output[0]), (normed_hidden_input, key_value_cotangents[:, 1], adapter_input_factors[2], key_value_adapter_output[1]), (attention_mixture, attention_out_cotangent, adapter_input_factors[3], adapter_output_factors[1]), (normed_gate_input, gate_up_cotangents[:, 0], adapter_input_factors[4], gate_up_adapter_output[0]), (normed_gate_input, gate_up_cotangents[:, 1], adapter_input_factors[5], gate_up_adapter_output[1]), (down_projection_input, down_out_cotangent, down_adapter_input_factor, adapter_output_factors[2])]
    col_keys = jnp.arange(K, dtype=jnp.int32) * -1640531535
    raw_sum = jnp.zeros((EXAMPLES, K), jnp.float32)
    for number, (inputs, cotangent, factor_a, factor_b) in enumerate(block_triplets):
        grad_a, grad_b = example_grads(inputs, cotangent, factor_a, factor_b, weights)
        keys_a = segment_keys(inputs.shape[1], block_projector_seeds[2 * number])
        keys_b = segment_keys(cotangent.shape[1], block_projector_seeds[2 * number + 1])
        raw_sum = raw_sum + project_rows(grad_a, keys_a, col_keys, 1024)
        raw_sum = raw_sum + project_rows(grad_b, keys_b, col_keys, 1024)
    scale_out = 1.0 / (LENGTH * math.sqrt(21845.0 * K))
    return raw_sum * scale_out
```

```python
import math

import jax
import jax.numpy as jnp
import numpy as np
from jax import lax
from jax.experimental import pallas as pl
from jax.experimental.pallas import tpu as pltpu
from jax.sharding import PartitionSpec as P

K = 2048
LENGTH = 2048
RANK = 8
ROWS = 256
SEED_MULT = 1103515245
ROW_MULT = 668265263
COL_MULT = -1640531535
MIX_A = -2048144789
MIX_B = -1028477387
STORED_STEPS = (4, 8, 10, 6, 4)

srl = lax.shift_right_logical


def chunk_of(width, unit, limit=4608):
    for parts in range(1, width // unit + 1):
        if width % (parts * unit) == 0 and width // parts <= limit:
            return width // parts
    return width


def wrapped(number):
    return (number + 2**31) % 2**32 - 2**31


def rows_of(parts):
    return jnp.concatenate(parts, axis=0) if len(parts) > 1 else parts[0]


class Plan:
    def __init__(self, widths, tokens, owners):
        self.widths = widths
        self.tokens = tokens
        self.owners = owners
        hid, att, gin, dwn, qry, kvw, aow, guw, dow = widths
        self.pieces = [
            (0, (24, 32, 40), (0, 2, 4), hid),
            (4, (0,), (1,), qry),
            (5, (8, 16), (3, 5), kvw),
            (1, (56,), (6,), att),
            (6, (48,), (7,), aow),
            (2, (80, 88), (8, 10), gin),
            (7, (64, 72), (9, 11), guw),
            (3, (104,), (12,), dwn),
            (8, (96,), (13,), dow),
        ]
        self.block = 0
        for _, _, _, width in self.pieces:
            self.block = math.gcd(self.block, width)
        while self.block > 512:
            self.block //= 2
        seg_tab, off_tab, width_tab = [], [], []
        self.first_block = {}
        for _, _, segs, width in self.pieces:
            for seg in segs:
                self.first_block[seg] = len(seg_tab)
                for number in range(width // self.block):
                    seg_tab.append(seg)
                    off_tab.append(number * self.block)
                    width_tab.append(width)
        self.blocks = len(seg_tab)
        self.table = np.array([seg_tab, off_tab, width_tab], np.int32)
        self.group = LENGTH // tokens
        self.examples = owners // self.group
        self.own_blocks = self.blocks // owners
        self.sub = min(ROWS, self.block)
        self.steps = self.own_blocks * (self.block // self.sub) * RANK
        bits = self.group.bit_length() - 1
        self.bits = ([0, 1] + list(reversed(range(2, bits))))[:bits]

    def first_own(self):
        j = lax.axis_index("proj")
        piece = 0
        for bit in self.bits:
            piece = piece * 2 + ((j >> bit) & 1)
        return piece * (self.blocks // self.group) + (j // self.group) * self.own_blocks


def product_kernel(plan):
    def kernel(*refs):
        data = refs[:9]
        aif, daf, aof, kvb, gub = refs[9:14]
        out = refs[14]
        bufs = refs[15:24]
        pairs = refs[24]
        sems = refs[25]
        order = [(0, lambda c: rows_of([aif[i, :, c] for i in (0, 1, 2)]), (0,)),
                 (4, lambda c: aof[0, :, c], (24,)),
                 (5, lambda c: rows_of([kvb[i, :, c] for i in (0, 1)]), (32, 40)),
                 (1, lambda c: aif[3, :, c], (48,)),
                 (6, lambda c: aof[1, :, c], (56,)),
                 (2, lambda c: rows_of([aif[i, :, c] for i in (4, 5)]), (64,)),
                 (7, lambda c: rows_of([gub[i, :, c] for i in (0, 1)]), (80, 88)),
                 (3, lambda c: daf[:, c], (96,)),
                 (8, lambda c: aof[2, :, c], (104,))]
        copies = []
        for arg, _, _ in order:
            width = plan.widths[arg]
            step = chunk_of(width, plan.block)
            for start in range(0, width, step):
                view = (slice(None),) * (len(data[arg].shape) - 1) + (pl.ds(start, step),)
                copies.append((arg, start, step, pltpu.make_async_copy(
                    data[arg].at[view], bufs[arg].at[view], sems.at[len(copies)])))
        for copy in copies:
            copy[3].start()
        for arg, factor, places in order:
            total = None
            for one, start, step, copy in copies:
                if one != arg:
                    continue
                copy.wait()
                cols = pl.ds(start, step)
                if len(data[arg].shape) == 3:
                    left = bufs[arg][:, :, cols].reshape(2 * plan.tokens, step)
                else:
                    left = bufs[arg][:, cols]
                part = lax.dot_general(left, factor(cols), (((1,), (1,)), ((), ())),
                                       preferred_element_type=jnp.float32)
                total = part if total is None else total + part
            if len(places) == 2:
                pairs[:, 0:2 * RANK] = total
                for i, place in enumerate(places):
                    got = pairs[pl.ds(i, plan.tokens, stride=2), :]
                    out[:, place:place + RANK] = got[:, i * RANK:(i + 1) * RANK]
            else:
                out[:, places[0]:places[0] + total.shape[1]] = total
        out[:, 112:] = jnp.zeros((plan.tokens, 16), jnp.float32)

    return kernel


def copy_count(plan):
    return sum(width // chunk_of(width, plan.block) for width in plan.widths)


def data_buffers(plan, data):
    return [pltpu.VMEM(x.shape, jnp.bfloat16) for x in data]


def products(plan, data, factors):
    anywhere = pl.BlockSpec(memory_space=pl.ANY)
    whole = pl.BlockSpec(memory_space=pltpu.VMEM)
    return pl.pallas_call(
        product_kernel(plan),
        in_specs=[anywhere] * 9 + [whole] * 5,
        out_specs=whole,
        out_shape=jax.ShapeDtypeStruct((plan.tokens, 128), jnp.float32),
        scratch_shapes=data_buffers(plan, data)
        + [pltpu.VMEM((2 * plan.tokens, 128), jnp.float32), pltpu.SemaphoreType.DMA((copy_count(plan),))],
        name="products",
    )(*data, *factors)


def gradient_kernel(plan, split):
    def kernel(*refs):
        data = refs[:9]
        own, other, mask = refs[9:12]
        keep, send = refs[12:14]
        bufs = refs[14:23]
        grads, sems, out_sems = refs[23:26]
        copies = {}
        number = 0
        for arg, _, _, width in plan.pieces:
            step = chunk_of(width, plan.block)
            for start in range(0, width, step):
                view = (slice(None),) * (len(data[arg].shape) - 1) + (pl.ds(start, step),)
                copies[arg, start] = pltpu.make_async_copy(data[arg].at[view], bufs[arg].at[view], sems.at[number])
                number += 1
        for copy in copies.values():
            copy.start()
        total = own[...] + other[...]
        turned = total.T * mask[...].astype(jnp.float32)
        tokens = plan.tokens
        half = plan.blocks // 2
        for arg, places, segs, width in plan.pieces:
            left = rows_of([turned[p:p + RANK] for p in places]).astype(jnp.bfloat16)
            if len(data[arg].shape) == 3:
                t = lax.broadcasted_iota(jnp.int32, (tokens, 2 * tokens), 0)
                u = lax.broadcasted_iota(jnp.int32, (tokens, 2 * tokens), 1)
                parts = []
                for i in range(2):
                    spread = (u == 2 * t + i).astype(jnp.float32).astype(jnp.bfloat16)
                    one = turned[places[i]:places[i] + RANK].astype(jnp.bfloat16)
                    parts.append(jnp.dot(one, spread, preferred_element_type=jnp.float32))
                left = rows_of(parts).astype(jnp.bfloat16)
            step = chunk_of(width, plan.block)
            for start in range(0, width, step):
                copies[arg, start].wait()
                cols = pl.ds(start, step)
                if len(data[arg].shape) == 3:
                    right = bufs[arg][:, :, cols].reshape(2 * tokens, step)
                else:
                    right = bufs[arg][:, cols]
                got = jnp.dot(left, right, preferred_element_type=jnp.float32)
                for i, seg in enumerate(segs):
                    for k in range(step // plan.block):
                        block = plan.first_block[seg] + start // plan.block + k
                        grads[block // half, block % half] = got[
                            i * RANK:(i + 1) * RANK, k * plan.block:(k + 1) * plan.block]
        bit = (lax.axis_index("proj") >> split) & 1
        first = pltpu.make_async_copy(grads.at[1 - bit], send, out_sems.at[0])
        second = pltpu.make_async_copy(grads.at[bit], keep, out_sems.at[1])
        first.start()
        second.start()
        first.wait()
        second.wait()

    return kernel


def gradients(plan, data, own, other, mask, split):
    anywhere = pl.BlockSpec(memory_space=pl.ANY)
    whole = pl.BlockSpec(memory_space=pltpu.VMEM)
    half = jax.ShapeDtypeStruct((plan.blocks // 2, RANK, plan.block), jnp.float32)
    return pl.pallas_call(
        gradient_kernel(plan, split),
        in_specs=[anywhere] * 9 + [whole] * 3,
        out_specs=[anywhere] * 2,
        out_shape=[half, half],
        scratch_shapes=data_buffers(plan, data)
        + [
            pltpu.VMEM((2, plan.blocks // 2, RANK, plan.block), jnp.float32),
            pltpu.SemaphoreType.DMA((copy_count(plan),)),
            pltpu.SemaphoreType.DMA((2,)),
        ],
        name="gradients",
    )(*data, own, other, mask)


def hashed(plan, step, seeds, table, columns):
    number = step // RANK
    rank = step % RANK
    parts = plan.block // plan.sub
    block = plan.first_own() + number // parts
    seg = table[0, block]
    feature = lax.axis_index("mp") * table[2, block] + table[1, block] + (number % parts) * plan.sub
    base = seeds[seg] * SEED_MULT + (feature * RANK + rank) * ROW_MULT
    key = base + lax.broadcasted_iota(jnp.int32, (plan.sub, 1), 0) * wrapped(RANK * ROW_MULT)
    return key ^ srl(key, 16)


def column_keys():
    cols = lax.broadcasted_iota(jnp.int32, (1, K), 1) * COL_MULT
    return cols ^ srl(cols, 16)


def mixed(rows, cols):
    h = (rows ^ cols) * MIX_A
    h = h ^ srl(h, 13)
    return h * MIX_B


def centred_sum(h):
    h = h ^ srl(h, 16)
    s = (h & 0x00FF00FF) + (srl(h, 8) | -0xFF0100)
    return (s * 0x10001).astype(jnp.float32).astype(jnp.bfloat16)


def byte_planes(h):
    low = h.astype(jnp.int16)
    high = srl(h, 16).astype(jnp.int16)
    low = low ^ high
    eight = jnp.int16(8)
    planes = [low, high, srl(low, eight), srl(high, eight)]
    return [p.astype(jnp.uint8).astype(jnp.bfloat16) for p in planes]


COLS = 256


def table_kernel(plan, first):
    def kernel(table, seeds, *refs):
        out = refs[-1]
        step = pl.program_id(0) + first
        columns = column_keys()
        rows = hashed(plan, step, seeds, table, columns)
        for c in range(0, K, COLS):
            out[0, :, c:c + COLS] = centred_sum(mixed(rows, columns[:, c:c + COLS]))

    return kernel


def stored_table(plan, table, seeds, first, count, total, after, so_far):
    smem = pl.BlockSpec(memory_space=pltpu.SMEM)
    anywhere = pl.BlockSpec(memory_space=pl.ANY)
    extra = [after] + ([so_far] if so_far is not None else [])
    return pl.pallas_call(
        table_kernel(plan, first),
        grid=(count,),
        in_specs=[smem, smem] + [anywhere] * len(extra),
        out_specs=pl.BlockSpec((1, plan.sub, K), lambda i: (i + first, 0, 0)),
        out_shape=jax.ShapeDtypeStruct((total, plan.sub, K), jnp.bfloat16),
        input_output_aliases={3: 0} if so_far is not None else {},
        name="stored_table",
    )(table, seeds, *extra)


def project_kernel(plan, stored, scale):
    fresh = plan.steps - stored
    depth = 2 * RANK * plan.examples

    def pick(grads, step):
        rank = step % RANK
        rows = lax.broadcasted_iota(jnp.int32, (RANK, plan.sub), 0) == rank
        parts = []
        for e in range(plan.examples):
            g = jnp.where(rows, grads[e, 0], 0.0)
            top = g.astype(jnp.bfloat16).astype(jnp.float32)
            parts += [top, g - top]
        return rows_of(parts).astype(jnp.bfloat16)

    def kernel(table, seeds, grads, old_grads, tiles, out, acc):
        i = pl.program_id(0)

        @pl.when(i == 0)
        def _():
            acc[...] = jnp.zeros_like(acc)

        columns = column_keys()
        rows = hashed(plan, i + stored, seeds, table, columns)
        left = pick(grads, i + stored)
        fix = -510.0 * jnp.sum(left.astype(jnp.float32), axis=1, keepdims=True)
        old = pick(old_grads, i)
        old = jnp.where(i < stored, old.astype(jnp.float32), 0.0)
        fix = fix + jnp.sum(old, axis=1, keepdims=True)
        old = (old * (1.0 / 65536.0)).astype(jnp.bfloat16)
        for c in range(0, K, COLS):
            a = acc[:, c:c + COLS] + fix
            for plane in byte_planes(mixed(rows, columns[:, c:c + COLS])):
                a = a + jnp.dot(left, plane, preferred_element_type=jnp.float32)
            a = a + jnp.dot(old, tiles[0, :, c:c + COLS], preferred_element_type=jnp.float32)
            acc[:, c:c + COLS] = a

        @pl.when(i == fresh - 1)
        def _():
            for e in range(plan.examples):
                part = acc[e * 2 * RANK:(e + 1) * 2 * RANK, :]
                out[e:e + 1, :] = jnp.sum(part, axis=0, keepdims=True) * scale

    return kernel, depth, fresh


def project(plan, table, seeds, grads, tiles, stored, scale):
    kernel, depth, fresh = project_kernel(plan, stored, scale)
    smem = pl.BlockSpec(memory_space=pltpu.SMEM)
    parts = plan.block // plan.sub

    def place(step):
        number = step // RANK
        return (0, number // parts, 0, number % parts)

    last = stored - 1
    return pl.pallas_call(
        kernel,
        grid=(fresh,),
        in_specs=[
            smem,
            smem,
            pl.BlockSpec((plan.examples, 1, RANK, plan.sub), lambda i: place(i + stored)),
            pl.BlockSpec((plan.examples, 1, RANK, plan.sub), lambda i: place(jnp.minimum(i, last))),
            pl.BlockSpec((1, plan.sub, K), lambda i: (jnp.minimum(i, last), 0, 0)),
        ],
        out_specs=pl.BlockSpec((plan.examples, K), lambda i: (0, 0)),
        out_shape=jax.ShapeDtypeStruct((plan.examples, K), jnp.float32),
        scratch_shapes=[pltpu.VMEM((depth, K), jnp.float32)],
        name="project",
    )(table, seeds, grads, grads, tiles)


def swap(x, axis, bit):
    size = lax.axis_size(axis)
    return lax.ppermute(x, axis, [(i, i ^ (1 << bit)) for i in range(size)])


def shards(*args):
    data = args[:9]
    factors = args[9:14]
    mask, seeds = args[14:16]
    plan = Plan(tuple(x.shape[-1] for x in data), data[0].shape[0], lax.axis_size("proj"))
    table = jnp.asarray(plan.table)
    counts = [max(1, c * plan.steps // 128) for c in STORED_STEPS][:1 + len(plan.bits)]
    stored = sum(counts)
    tiles = None
    first = 0

    def cover(received, sent, number):
        nonlocal tiles, first
        tiles = stored_table(plan, table, seeds, first, counts[number], stored, sent, tiles)
        first += counts[number]
        received, tiles = lax.optimization_barrier((received, tiles))
        return received

    own = products(plan, data, factors)
    if lax.axis_size("mp") == 2:
        other = swap(own, "mp", 0)
    else:
        own = lax.psum(own, "mp")
        other = jnp.zeros_like(own)
    other = cover(other, own, 0)
    keep, send = gradients(plan, data, own, other, mask.reshape(1, -1), plan.bits[0])
    j = lax.axis_index("proj")
    x = None
    for number, bit in enumerate(plan.bits):
        if number > 0:
            half = x.shape[0] // 2
            side = (j >> bit) & 1
            send = lax.dynamic_slice_in_dim(x, (1 - side) * half, half, 0)
            keep = lax.dynamic_slice_in_dim(x, side * half, half, 0)
        received = cover(swap(send, "proj", bit), send, number + 1)
        x = keep + received
    x = x[None]
    if plan.examples > 1:
        groups = [[e * plan.group + i for e in range(plan.examples)] for i in range(plan.group)]
        x = x.reshape((plan.examples, plan.own_blocks) + x.shape[2:])
        x = lax.all_to_all(x, "proj", 0, 0, axis_index_groups=groups, tiled=True)
    scale = 1.0 / (LENGTH * math.sqrt(21845.0 * K))
    partial = project(plan, table, seeds, x, tiles, stored, scale)
    devices = lax.axis_size("mp") * plan.owners
    pieces = partial.reshape(plan.examples, devices, K // devices).transpose(1, 0, 2)
    got = lax.all_to_all(pieces, ("mp", "proj"), 0, 0, tiled=True)
    return got.sum(axis=0)


def solution(mesh):
    in_specs = (
        P("proj", "mp"),
        P("proj", "mp"),
        P("proj", "mp"),
        P("proj", "mp"),
        P("proj", "mp"),
        P("proj", None, "mp"),
        P("proj", "mp"),
        P("proj", None, "mp"),
        P("proj", "mp"),
        P(None, None, "mp"),
        P(None, "mp"),
        P(None, None, "mp"),
        P(None, None, "mp"),
        P(None, None, "mp"),
        P("proj"),
        P(),
    )
    out_specs = P(None, ("mp", "proj"))
    return jax.shard_map(shards, mesh=mesh, in_specs=in_specs, out_specs=out_specs, check_vma=False)
```

```python
import math

import jax
import jax.numpy as jnp
import numpy as np
from jax import lax
from jax.experimental import pallas as pl
from jax.experimental.pallas import tpu as pltpu
from jax.sharding import PartitionSpec as P

K = 2048
LENGTH = 2048
RANK = 8
ROWS = 256
SEED_MULT = 1103515245
ROW_MULT = 668265263
COL_MULT = -1640531535
MIX_A = -2048144789
MIX_B = -1028477387
STORED_STEPS = (6, 3, 5, 6, 10, 7, 3)

srl = lax.shift_right_logical


def chunk_of(width, unit, limit=4608):
    for parts in range(1, width // unit + 1):
        if width % (parts * unit) == 0 and width // parts <= limit:
            return width // parts
    return width


def wrapped(number):
    return (number + 2**31) % 2**32 - 2**31


def rows_of(parts):
    return jnp.concatenate(parts, axis=0) if len(parts) > 1 else parts[0]


class Plan:
    def __init__(self, widths, tokens, owners):
        self.widths = widths
        self.tokens = tokens
        self.owners = owners
        hid, att, gin, dwn, qry, kvw, aow, guw, dow = widths
        self.pieces = [
            (0, (24, 32, 40), (0, 2, 4), hid),
            (4, (0,), (1,), qry),
            (5, (8, 16), (3, 5), kvw),
            (1, (56,), (6,), att),
            (6, (48,), (7,), aow),
            (2, (80, 88), (8, 10), gin),
            (7, (64, 72), (9, 11), guw),
            (3, (104,), (12,), dwn),
            (8, (96,), (13,), dow),
        ]
        self.block = 0
        for _, _, _, width in self.pieces:
            self.block = math.gcd(self.block, width)
        while self.block > 512:
            self.block //= 2
        seg_tab, off_tab, width_tab = [], [], []
        self.first_block = {}
        for _, _, segs, width in self.pieces:
            for seg in segs:
                self.first_block[seg] = len(seg_tab)
                for number in range(width // self.block):
                    seg_tab.append(seg)
                    off_tab.append(number * self.block)
                    width_tab.append(width)
        self.blocks = len(seg_tab)
        self.table = np.array([seg_tab, off_tab, width_tab], np.int32)
        self.group = LENGTH // tokens
        self.examples = owners // self.group
        self.own_blocks = self.blocks // owners
        self.sub = min(ROWS, self.block)
        self.steps = self.own_blocks * (self.block // self.sub) * RANK
        bits = self.group.bit_length() - 1
        self.bits = ([0, 1] + list(reversed(range(2, bits))))[:bits]

    def first_own(self):
        j = lax.axis_index("proj")
        piece = 0
        for bit in self.bits:
            piece = piece * 2 + ((j >> bit) & 1)
        return piece * (self.blocks // self.group) + (j // self.group) * self.own_blocks


def product_kernel(plan, count):
    def kernel(*refs):
        data = refs[:9]
        weights = refs[9:14]
        fill_refs = refs[14:16]
        out, tiles = refs[16:18]
        bufs = refs[18:27]
        pairs, sems = refs[27:29]
        factor_bufs = refs[29:34]
        aif, daf, aof, kvb, gub = factor_bufs
        fill_refs = fill_refs + refs[34:]
        order = [(0, lambda c: rows_of([aif[i, :, c] for i in (0, 1, 2)]), (0,)),
                 (4, lambda c: aof[0, :, c], (24,)),
                 (5, lambda c: rows_of([kvb[i, :, c] for i in (0, 1)]), (32, 40)),
                 (1, lambda c: aif[3, :, c], (48,)),
                 (6, lambda c: aof[1, :, c], (56,)),
                 (2, lambda c: rows_of([aif[i, :, c] for i in (4, 5)]), (64,)),
                 (7, lambda c: rows_of([gub[i, :, c] for i in (0, 1)]), (80, 88)),
                 (3, lambda c: daf[:, c], (96,)),
                 (8, lambda c: aof[2, :, c], (104,))]
        copies = []
        for arg, _, _ in order:
            width = plan.widths[arg]
            step = chunk_of(width, plan.block)
            for start in range(0, width, step):
                view = (slice(None),) * (len(data[arg].shape) - 1) + (pl.ds(start, step),)
                copies.append((arg, start, step, pltpu.make_async_copy(
                    data[arg].at[view], bufs[arg].at[view], sems.at[len(copies)])))
        loads = [pltpu.make_async_copy(weights[i], factor_bufs[i], sems.at[len(copies) + i]) for i in range(5)]
        for copy in loads + [copy[3] for copy in copies]:
            copy.start()
        finish = fill_tables(plan, 0, count, fill_refs, tiles)
        for load in loads:
            load.wait()
        for arg, factor, places in order:
            total = None
            for one, start, step, copy in copies:
                if one != arg:
                    continue
                copy.wait()
                cols = pl.ds(start, step)
                if len(data[arg].shape) == 3:
                    left = bufs[arg][:, :, cols].reshape(2 * plan.tokens, step)
                else:
                    left = bufs[arg][:, cols]
                part = lax.dot_general(left, factor(cols), (((1,), (1,)), ((), ())),
                                       preferred_element_type=jnp.float32)
                total = part if total is None else total + part
            if len(places) == 2:
                pairs[:, 0:2 * RANK] = total
                for i, place in enumerate(places):
                    got = pairs[pl.ds(i, plan.tokens, stride=2), :]
                    out[:, place:place + RANK] = got[:, i * RANK:(i + 1) * RANK]
            else:
                out[:, places[0]:places[0] + total.shape[1]] = total
        out[:, 112:] = jnp.zeros((plan.tokens, 16), jnp.float32)
        finish()

    return kernel


def copy_count(plan):
    return sum(width // chunk_of(width, plan.block) for width in plan.widths)


def data_buffers(plan, data):
    return [pltpu.VMEM(x.shape, jnp.bfloat16) for x in data]


def products(plan, data, factors, table, seeds, count, total):
    anywhere = pl.BlockSpec(memory_space=pl.ANY)
    smem = pl.BlockSpec(memory_space=pltpu.SMEM)
    whole = pl.BlockSpec(memory_space=pltpu.VMEM)
    return pl.pallas_call(
        product_kernel(plan, count),
        in_specs=[anywhere] * 14 + [smem, smem],
        out_specs=[whole, anywhere],
        out_shape=[jax.ShapeDtypeStruct((plan.tokens, 128), jnp.float32), tiles_shape(plan, total)],
        scratch_shapes=data_buffers(plan, data)
        + [pltpu.VMEM((2 * plan.tokens, 128), jnp.float32), pltpu.SemaphoreType.DMA((copy_count(plan) + 5,))]
        + [pltpu.VMEM(x.shape, x.dtype) for x in factors]
        + fill_scratch(plan, count),
        name="products",
    )(*data, *factors, table, seeds)


def gradient_kernel(plan, split, first, count):
    def kernel(*refs):
        data = refs[:9]
        own, other, mask = refs[9:12]
        fill_refs = refs[12:14]
        keep, send, tiles = refs[15:18]
        bufs = refs[18:27]
        grads, sems, out_sems = refs[27:30]
        fill_refs = fill_refs + refs[30:]
        copies = {}
        number = 0
        for arg, _, _, width in plan.pieces:
            step = chunk_of(width, plan.block)
            for start in range(0, width, step):
                view = (slice(None),) * (len(data[arg].shape) - 1) + (pl.ds(start, step),)
                copies[arg, start] = pltpu.make_async_copy(data[arg].at[view], bufs[arg].at[view], sems.at[number])
                number += 1
        for copy in copies.values():
            copy.start()
        finish = fill_tables(plan, first, count, fill_refs, tiles)
        total = own[...] + other[...]
        turned = total.T * mask[...].astype(jnp.float32)
        tokens = plan.tokens
        half = plan.blocks // 2
        for arg, places, segs, width in plan.pieces:
            left = rows_of([turned[p:p + RANK] for p in places]).astype(jnp.bfloat16)
            if len(data[arg].shape) == 3:
                t = lax.broadcasted_iota(jnp.int32, (tokens, 2 * tokens), 0)
                u = lax.broadcasted_iota(jnp.int32, (tokens, 2 * tokens), 1)
                parts = []
                for i in range(2):
                    spread = (u == 2 * t + i).astype(jnp.float32).astype(jnp.bfloat16)
                    one = turned[places[i]:places[i] + RANK].astype(jnp.bfloat16)
                    parts.append(jnp.dot(one, spread, preferred_element_type=jnp.float32))
                left = rows_of(parts).astype(jnp.bfloat16)
            step = chunk_of(width, plan.block)
            for start in range(0, width, step):
                copies[arg, start].wait()
                cols = pl.ds(start, step)
                if len(data[arg].shape) == 3:
                    right = bufs[arg][:, :, cols].reshape(2 * tokens, step)
                else:
                    right = bufs[arg][:, cols]
                got = jnp.dot(left, right, preferred_element_type=jnp.float32)
                for i, seg in enumerate(segs):
                    for k in range(step // plan.block):
                        block = plan.first_block[seg] + start // plan.block + k
                        grads[block // half, block % half] = got[
                            i * RANK:(i + 1) * RANK, k * plan.block:(k + 1) * plan.block]
        bit = (lax.axis_index("proj") >> split) & 1
        sent = pltpu.make_async_copy(grads.at[1 - bit], send, out_sems.at[0])
        kept = pltpu.make_async_copy(grads.at[bit], keep, out_sems.at[1])
        sent.start()
        kept.start()
        finish()
        sent.wait()
        kept.wait()

    return kernel


def gradients(plan, data, own, other, mask, split, table, seeds, first, count, so_far):
    anywhere = pl.BlockSpec(memory_space=pl.ANY)
    smem = pl.BlockSpec(memory_space=pltpu.SMEM)
    whole = pl.BlockSpec(memory_space=pltpu.VMEM)
    half = jax.ShapeDtypeStruct((plan.blocks // 2, RANK, plan.block), jnp.float32)
    return pl.pallas_call(
        gradient_kernel(plan, split, first, count),
        in_specs=[anywhere] * 9 + [whole] * 3 + [smem, smem, anywhere],
        out_specs=[anywhere] * 3,
        out_shape=[half, half, jax.ShapeDtypeStruct(so_far.shape, so_far.dtype)],
        scratch_shapes=data_buffers(plan, data)
        + [
            pltpu.VMEM((2, plan.blocks // 2, RANK, plan.block), jnp.float32),
            pltpu.SemaphoreType.DMA((copy_count(plan),)),
            pltpu.SemaphoreType.DMA((2,)),
        ]
        + fill_scratch(plan, count),
        input_output_aliases={14: 2},
        name="gradients",
    )(*data, own, other, mask, table, seeds, so_far)


def row_offsets(plan):
    return lax.broadcasted_iota(jnp.int32, (plan.sub, COLS), 0) * wrapped(RANK * ROW_MULT)


def step_keys(plan, step, seeds, table, offsets):
    number = step // RANK
    rank = step % RANK
    parts = plan.block // plan.sub
    block = plan.first_own() + number // parts
    seg = table[0, block]
    feature = lax.axis_index("mp") * table[2, block] + table[1, block] + (number % parts) * plan.sub
    base = seeds[seg] * SEED_MULT + (feature * RANK + rank) * ROW_MULT
    key = base + offsets
    return key ^ srl(key, 16)


def column_keys(copies=1):
    cols = lax.broadcasted_iota(jnp.int32, (copies, K), 1) * COL_MULT
    return cols ^ srl(cols, 16)


def mixed(rows, cols):
    shape = rows.shape[0], cols.shape[1]
    h = rows.reshape(shape[0] // RANK, RANK, rows.shape[1]) ^ cols[None]
    h = h.reshape(shape) * MIX_A
    h = h ^ srl(h, 13)
    return h * MIX_B


def centred_sum(h):
    h = h ^ srl(h, 16)
    s = (h & 0x00FF00FF) + (srl(h, 8) | -0xFF0100)
    return (s * 0x10001).astype(jnp.float32).astype(jnp.bfloat16)


def byte_planes(h):
    low = h.astype(jnp.int16)
    high = srl(h, 16).astype(jnp.int16)
    low = low ^ high
    eight = jnp.int16(8)
    planes = [low, high, srl(low, eight), srl(high, eight)]
    return [p.astype(jnp.uint8).astype(jnp.bfloat16) for p in planes]


COLS = 256
LANES = 128


def fill_step(plan, step, seeds, table, row_base, col_base, tile):
    rows = step_keys(plan, step, seeds, table, row_base[...])
    for c in range(0, K, COLS):
        part = centred_sum(mixed(rows, col_base[:, c:c + COLS]))
        for n in range(0, COLS, LANES):
            tile[(c + n) // LANES] = part[:, n:n + LANES]


def fill_tables(plan, first, count, refs, out):
    table, seeds, row_base, col_base, tiles, sems = refs
    row_base[...] = row_offsets(plan)
    col_base[...] = column_keys(RANK)

    def body(n, carry):
        fill_step(plan, n + first, seeds, table, row_base, col_base, tiles.at[n])
        pltpu.make_async_copy(tiles.at[n], out.at[n + first], sems.at[n]).start()
        return carry

    lax.fori_loop(0, count, body, 0)

    def wait():
        for n in range(count):
            pltpu.make_async_copy(tiles.at[n], out.at[n + first], sems.at[n]).wait()

    return wait


def fill_scratch(plan, count):
    return [
        pltpu.VMEM((plan.sub, COLS), jnp.int32),
        pltpu.VMEM((RANK, K), jnp.int32),
        pltpu.VMEM((count, K // LANES, plan.sub, LANES), jnp.bfloat16),
        pltpu.SemaphoreType.DMA((count,)),
    ]


def tiles_shape(plan, total):
    return jax.ShapeDtypeStruct((total, K // LANES, plan.sub, LANES), jnp.bfloat16)


def stored_table(plan, table, seeds, first, count, after, so_far):
    smem = pl.BlockSpec(memory_space=pltpu.SMEM)
    anywhere = pl.BlockSpec(memory_space=pl.ANY)

    def kernel(table, seeds, after, so_far, out, *scratch):
        fill_tables(plan, first, count, (table, seeds) + scratch, out)()

    return pl.pallas_call(
        kernel,
        in_specs=[smem, smem, anywhere, anywhere],
        out_specs=anywhere,
        out_shape=jax.ShapeDtypeStruct(so_far.shape, so_far.dtype),
        scratch_shapes=fill_scratch(plan, count),
        input_output_aliases={3: 0},
        name="stored_table",
    )(table, seeds, after, so_far)


def project_kernel(plan, stored, scale, devices):
    fresh = plan.steps - stored
    depth = 2 * RANK * plan.examples
    parts = 4
    slab = plan.sub // parts

    def pick(grads, step):
        rank = step % RANK
        rows = lax.broadcasted_iota(jnp.int32, (RANK, plan.sub), 0) == rank
        parts = []
        for e in range(plan.examples):
            g = jnp.where(rows, grads[e, 0], 0.0)
            top = g.astype(jnp.bfloat16).astype(jnp.float32)
            parts += [top, g - top]
        return rows_of(parts).astype(jnp.bfloat16)

    def kernel(table, seeds, grads, old_grads, tiles, out, acc, row_base, col_base):
        i = pl.program_id(0)

        @pl.when(i == 0)
        def _():
            acc[...] = jnp.zeros_like(acc)
            row_base[...] = row_offsets(plan)
            col_base[...] = column_keys(RANK)

        rows = step_keys(plan, i + stored, seeds, table, row_base[...])
        left = pick(grads, i + stored)
        fix = -510.0 * jnp.sum(left.astype(jnp.float32), axis=1, keepdims=True)
        old = pick(old_grads, i)
        old = jnp.where(i < stored, old.astype(jnp.float32), 0.0)
        fix = fix + jnp.sum(old, axis=1, keepdims=True)
        old = (old * (1.0 / 65536.0)).astype(jnp.bfloat16)
        lefts = [jnp.concatenate([left[:, b:b + slab]] * parts, axis=1) for b in range(0, plan.sub, slab)]
        for c in range(0, K, COLS):
            a = acc[:, c:c + COLS] + fix
            for n in range(parts):
                planes = byte_planes(mixed(rows[n * slab:(n + 1) * slab], col_base[:, c:c + COLS]))
                a = a + jnp.dot(lefts[n], rows_of(planes), preferred_element_type=jnp.float32)
            tile = jnp.concatenate([tiles[0, (c + n) // LANES] for n in range(0, COLS, LANES)], axis=1)
            a = a + jnp.dot(old, tile, preferred_element_type=jnp.float32)
            acc[:, c:c + COLS] = a

        @pl.when(i == fresh - 1)
        def _():
            width = K // devices
            for e in range(plan.examples):
                part = acc[e * 2 * RANK:(e + 1) * 2 * RANK, :]
                total = jnp.sum(part, axis=0, keepdims=True) * scale
                for d in range(devices):
                    out[d, e:e + 1, :] = total[:, d * width:(d + 1) * width]

    return kernel, depth, fresh


def project(plan, table, seeds, grads, tiles, stored, scale, devices):
    kernel, depth, fresh = project_kernel(plan, stored, scale, devices)
    smem = pl.BlockSpec(memory_space=pltpu.SMEM)
    parts = plan.block // plan.sub

    def place(step):
        number = step // RANK
        return (0, number // parts, 0, number % parts)

    last = stored - 1
    return pl.pallas_call(
        kernel,
        grid=(fresh,),
        in_specs=[
            smem,
            smem,
            pl.BlockSpec((plan.examples, 1, RANK, plan.sub), lambda i: place(i + stored)),
            pl.BlockSpec((plan.examples, 1, RANK, plan.sub), lambda i: place(jnp.minimum(i, last))),
            pl.BlockSpec((1, K // LANES, plan.sub, LANES), lambda i: (jnp.minimum(i, last), 0, 0, 0)),
        ],
        out_specs=pl.BlockSpec((devices, plan.examples, K // devices), lambda i: (0, 0, 0)),
        out_shape=jax.ShapeDtypeStruct((devices, plan.examples, K // devices), jnp.float32),
        scratch_shapes=[
            pltpu.VMEM((depth, K), jnp.float32),
            pltpu.VMEM((plan.sub, COLS), jnp.int32),
            pltpu.VMEM((RANK, K), jnp.int32),
        ],
        name="project",
    )(table, seeds, grads, grads, tiles)


def swap(x, axis, bit):
    size = lax.axis_size(axis)
    return lax.ppermute(x, axis, [(i, i ^ (1 << bit)) for i in range(size)])


def shards(*args):
    data = args[:9]
    factors = args[9:14]
    mask, seeds = args[14:16]
    plan = Plan(tuple(x.shape[-1] for x in data), data[0].shape[0], lax.axis_size("proj"))
    table = jnp.asarray(plan.table)
    counts = [max(1, c * plan.steps // 128) for c in STORED_STEPS][:3 + len(plan.bits)]
    starts = [sum(counts[:n]) for n in range(len(counts))]
    stored = sum(counts)
    own, tiles = products(plan, data, factors, table, seeds, counts[0], stored)

    def cover(received, sent, number):
        nonlocal tiles
        tiles = stored_table(plan, table, seeds, starts[number], counts[number], sent, tiles)
        received, tiles = lax.optimization_barrier((received, tiles))
        return received

    if lax.axis_size("mp") == 2:
        other = swap(own, "mp", 0)
    else:
        own = lax.psum(own, "mp")
        other = jnp.zeros_like(own)
    other = cover(other, own, 1)
    keep, send, tiles = gradients(
        plan, data, own, other, mask.reshape(1, -1), plan.bits[0], table, seeds, starts[2], counts[2], tiles)
    j = lax.axis_index("proj")
    x = None
    for number, bit in enumerate(plan.bits):
        if number > 0:
            half = x.shape[0] // 2
            side = (j >> bit) & 1
            send = lax.dynamic_slice_in_dim(x, (1 - side) * half, half, 0)
            keep = lax.dynamic_slice_in_dim(x, side * half, half, 0)
        received = cover(swap(send, "proj", bit), send, number + 3)
        x = keep + received
    x = x[None]
    if plan.examples > 1:
        groups = [[e * plan.group + i for e in range(plan.examples)] for i in range(plan.group)]
        x = x.reshape((plan.examples, plan.own_blocks) + x.shape[2:])
        x = lax.all_to_all(x, "proj", 0, 0, axis_index_groups=groups, tiled=True)
    scale = 1.0 / (LENGTH * math.sqrt(21845.0 * K))
    devices = lax.axis_size("mp") * plan.owners
    pieces = project(plan, table, seeds, x, tiles, stored, scale, devices)
    got = lax.all_to_all(pieces, ("mp", "proj"), 0, 0, tiled=True)
    return got.sum(axis=0)


def solution(mesh):
    in_specs = (
        P("proj", "mp"),
        P("proj", "mp"),
        P("proj", "mp"),
        P("proj", "mp"),
        P("proj", "mp"),
        P("proj", None, "mp"),
        P("proj", "mp"),
        P("proj", None, "mp"),
        P("proj", "mp"),
        P(None, None, "mp"),
        P(None, "mp"),
        P(None, None, "mp"),
        P(None, None, "mp"),
        P(None, None, "mp"),
        P("proj"),
        P(),
    )
    out_specs = P(None, ("mp", "proj"))
    return jax.shard_map(shards, mesh=mesh, in_specs=in_specs, out_specs=out_specs, check_vma=False)
```

```python
import math

import jax
import jax.numpy as jnp
import numpy as np
from jax import lax
from jax.experimental import pallas as pl
from jax.experimental.pallas import tpu as pltpu
from jax.sharding import PartitionSpec as P

K = 2048
LENGTH = 2048
RANK = 8
ROWS = 256
SEED_MULT = 1103515245
ROW_MULT = 668265263
COL_MULT = -1640531535
MIX_A = -2048144789
MIX_B = -1028477387
STORED_STEPS = (6, 2, 5, 5, 11, 10, 3)

srl = lax.shift_right_logical


def chunk_of(width, unit, limit=4608):
    for parts in range(1, width // unit + 1):
        if width % (parts * unit) == 0 and width // parts <= limit:
            return width // parts
    return width


def wrapped(number):
    return (number + 2**31) % 2**32 - 2**31


def rows_of(parts):
    return jnp.concatenate(parts, axis=0) if len(parts) > 1 else parts[0]


class Plan:
    def __init__(self, widths, tokens, owners):
        self.widths = widths
        self.tokens = tokens
        self.owners = owners
        hid, att, gin, dwn, qry, kvw, aow, guw, dow = widths
        self.pieces = [
            (0, (24, 32, 40), (0, 2, 4), hid),
            (4, (0,), (1,), qry),
            (5, (8, 16), (3, 5), kvw),
            (1, (56,), (6,), att),
            (6, (48,), (7,), aow),
            (2, (80, 88), (8, 10), gin),
            (7, (64, 72), (9, 11), guw),
            (3, (104,), (12,), dwn),
            (8, (96,), (13,), dow),
        ]
        self.block = 0
        for _, _, _, width in self.pieces:
            self.block = math.gcd(self.block, width)
        while self.block > 512:
            self.block //= 2
        seg_tab, off_tab, width_tab = [], [], []
        self.first_block = {}
        for _, _, segs, width in self.pieces:
            for seg in segs:
                self.first_block[seg] = len(seg_tab)
                for number in range(width // self.block):
                    seg_tab.append(seg)
                    off_tab.append(number * self.block)
                    width_tab.append(width)
        self.blocks = len(seg_tab)
        self.table = np.array([seg_tab, off_tab, width_tab], np.int32)
        self.group = LENGTH // tokens
        self.examples = owners // self.group
        self.own_blocks = self.blocks // owners
        self.sub = min(ROWS, self.block)
        self.steps = self.own_blocks * (self.block // self.sub) * RANK
        bits = self.group.bit_length() - 1
        self.bits = ([0, 1] + list(reversed(range(2, bits))))[:bits]

    def first_own(self):
        j = lax.axis_index("proj")
        piece = 0
        for bit in self.bits:
            piece = piece * 2 + ((j >> bit) & 1)
        return piece * (self.blocks // self.group) + (j // self.group) * self.own_blocks


def every_other(x, first):
    wide = x.shape[1]
    u = lax.broadcasted_iota(jnp.int32, (wide, wide // 2), 0)
    t = lax.broadcasted_iota(jnp.int32, (wide, wide // 2), 1)
    choose = (u == 2 * t + first).astype(jnp.float32).astype(jnp.bfloat16)
    total = None
    for _ in range(3):
        term = x.astype(jnp.bfloat16)
        x = x - term.astype(jnp.float32)
        got = jnp.dot(term, choose, preferred_element_type=jnp.float32)
        total = got if total is None else total + got
    return total


def product_kernel(plan, count):
    def kernel(*refs):
        data = refs[:9]
        weights = refs[9:14]
        fill_refs = refs[14:16]
        out, tiles, bases = refs[16:19]
        bufs = refs[19:28]
        sems = refs[28]
        factor_bufs = refs[29:34]
        aif, daf, aof, kvb, gub = factor_bufs
        table, seeds = fill_refs
        order = [(0, lambda c: rows_of([aif[i, :, c] for i in (0, 1, 2)]), (0,)),
                 (4, lambda c: aof[0, :, c], (24,)),
                 (5, lambda c: rows_of([kvb[i, :, c] for i in (0, 1)]), (32, 40)),
                 (1, lambda c: aif[3, :, c], (48,)),
                 (6, lambda c: aof[1, :, c], (56,)),
                 (2, lambda c: rows_of([aif[i, :, c] for i in (4, 5)]), (64,)),
                 (7, lambda c: rows_of([gub[i, :, c] for i in (0, 1)]), (80, 88)),
                 (3, lambda c: daf[:, c], (96,)),
                 (8, lambda c: aof[2, :, c], (104,))]
        copies = []
        for arg, _, _ in order:
            width = plan.widths[arg]
            step = chunk_of(width, plan.block)
            for start in range(0, width, step):
                view = (slice(None),) * (len(data[arg].shape) - 1) + (pl.ds(start, step),)
                copies.append((arg, start, step, pltpu.make_async_copy(
                    data[arg].at[view], bufs[arg].at[view], sems.at[len(copies)])))
        loads = [pltpu.make_async_copy(weights[i], factor_bufs[i], sems.at[len(copies) + i]) for i in range(5)]
        for copy in loads + [copy[3] for copy in copies]:
            copy.start()
        block = plan.first_own()
        for n in range(plan.steps // RANK):
            parts = plan.block // plan.sub
            seg = table[0, block + n // parts]
            feature = lax.axis_index("mp") * table[2, block + n // parts] + table[1, block + n // parts]
            feature = feature + (n % parts) * plan.sub
            bases[n] = seeds[seg] * SEED_MULT + feature * wrapped(RANK * ROW_MULT)
        finish = fill_tables(plan, 0, count, (bases,) + refs[34:], tiles)
        for load in loads:
            load.wait()
        for arg, factor, places in order:
            total = None
            for one, start, step, copy in copies:
                if one != arg:
                    continue
                copy.wait()
                cols = pl.ds(start, step)
                if len(data[arg].shape) == 3:
                    right = bufs[arg][:, :, cols].reshape(2 * plan.tokens, step)
                else:
                    right = bufs[arg][:, cols]
                part = lax.dot_general(factor(cols), right, (((1,), (1,)), ((), ())),
                                       preferred_element_type=jnp.float32)
                total = part if total is None else total + part
            if len(places) == 2:
                for i, place in enumerate(places):
                    out[place:place + RANK, :] = every_other(total[i * RANK:(i + 1) * RANK], i)
            else:
                out[places[0]:places[0] + total.shape[0], :] = total
        finish()

    return kernel


def copy_count(plan):
    return sum(width // chunk_of(width, plan.block) for width in plan.widths)


def data_buffers(plan, data):
    return [pltpu.VMEM(x.shape, jnp.bfloat16) for x in data]


def products(plan, data, factors, table, seeds, count, total):
    anywhere = pl.BlockSpec(memory_space=pl.ANY)
    smem = pl.BlockSpec(memory_space=pltpu.SMEM)
    whole = pl.BlockSpec(memory_space=pltpu.VMEM)
    return pl.pallas_call(
        product_kernel(plan, count),
        in_specs=[anywhere] * 14 + [smem, smem],
        out_specs=[whole, anywhere, smem],
        out_shape=[
            jax.ShapeDtypeStruct((14 * RANK, plan.tokens), jnp.float32),
            tiles_shape(plan, total),
            jax.ShapeDtypeStruct((plan.steps // RANK,), jnp.int32),
        ],
        scratch_shapes=data_buffers(plan, data)
        + [pltpu.SemaphoreType.DMA((copy_count(plan) + 5,))]
        + [pltpu.VMEM(x.shape, x.dtype) for x in factors]
        + fill_scratch(plan, count),
        name="products",
    )(*data, *factors, table, seeds)


def gradient_kernel(plan, split, first, count):
    def kernel(*refs):
        data = refs[:9]
        own, other, mask = refs[9:12]
        bases = refs[12]
        keep, send, tiles = refs[14:17]
        bufs = refs[17:26]
        grads, sems, out_sems = refs[26:29]
        fill_refs = (bases,) + refs[29:]
        copies = {}
        number = 0
        for arg, _, _, width in plan.pieces:
            step = chunk_of(width, plan.block)
            for start in range(0, width, step):
                view = (slice(None),) * (len(data[arg].shape) - 1) + (pl.ds(start, step),)
                copies[arg, start] = pltpu.make_async_copy(data[arg].at[view], bufs[arg].at[view], sems.at[number])
                number += 1
        for copy in copies.values():
            copy.start()
        finish = fill_tables(plan, first, count, fill_refs, tiles)
        total = own[...] + other[...]
        turned = total * mask[...].astype(jnp.float32)
        tokens = plan.tokens
        half = plan.blocks // 2
        for arg, places, segs, width in plan.pieces:
            left = rows_of([turned[p:p + RANK] for p in places]).astype(jnp.bfloat16)
            if len(data[arg].shape) == 3:
                t = lax.broadcasted_iota(jnp.int32, (tokens, 2 * tokens), 0)
                u = lax.broadcasted_iota(jnp.int32, (tokens, 2 * tokens), 1)
                parts = []
                for i in range(2):
                    spread = (u == 2 * t + i).astype(jnp.float32).astype(jnp.bfloat16)
                    one = turned[places[i]:places[i] + RANK].astype(jnp.bfloat16)
                    parts.append(jnp.dot(one, spread, preferred_element_type=jnp.float32))
                left = rows_of(parts).astype(jnp.bfloat16)
            step = chunk_of(width, plan.block)
            for start in range(0, width, step):
                copies[arg, start].wait()
                cols = pl.ds(start, step)
                if len(data[arg].shape) == 3:
                    right = bufs[arg][:, :, cols].reshape(2 * tokens, step)
                else:
                    right = bufs[arg][:, cols]
                got = jnp.dot(left, right, preferred_element_type=jnp.float32)
                for i, seg in enumerate(segs):
                    for k in range(step // plan.block):
                        block = plan.first_block[seg] + start // plan.block + k
                        grads[block // half, block % half] = got[
                            i * RANK:(i + 1) * RANK, k * plan.block:(k + 1) * plan.block]
        bit = (lax.axis_index("proj") >> split) & 1
        sent = pltpu.make_async_copy(grads.at[1 - bit], send, out_sems.at[0])
        kept = pltpu.make_async_copy(grads.at[bit], keep, out_sems.at[1])
        sent.start()
        kept.start()
        finish()
        sent.wait()
        kept.wait()

    return kernel


def gradients(plan, data, own, other, mask, split, bases, first, count, so_far):
    anywhere = pl.BlockSpec(memory_space=pl.ANY)
    smem = pl.BlockSpec(memory_space=pltpu.SMEM)
    whole = pl.BlockSpec(memory_space=pltpu.VMEM)
    half = jax.ShapeDtypeStruct((plan.blocks // 2, RANK, plan.block), jnp.float32)
    return pl.pallas_call(
        gradient_kernel(plan, split, first, count),
        in_specs=[anywhere] * 9 + [whole] * 3 + [smem, anywhere],
        out_specs=[anywhere] * 3,
        out_shape=[half, half, jax.ShapeDtypeStruct(so_far.shape, so_far.dtype)],
        scratch_shapes=data_buffers(plan, data)
        + [
            pltpu.VMEM((2, plan.blocks // 2, RANK, plan.block), jnp.float32),
            pltpu.SemaphoreType.DMA((copy_count(plan),)),
            pltpu.SemaphoreType.DMA((2,)),
        ]
        + fill_scratch(plan, count),
        input_output_aliases={13: 2},
        name="gradients",
    )(*data, own, other, mask, bases, so_far)


def row_offsets(plan):
    return lax.broadcasted_iota(jnp.int32, (plan.sub, COLS), 0) * wrapped(RANK * ROW_MULT)


def step_keys(step, bases, offsets):
    key = bases[step // RANK] + (step % RANK) * ROW_MULT + offsets
    return key ^ srl(key, 16)


def column_keys(copies=1):
    cols = lax.broadcasted_iota(jnp.int32, (copies, K), 1) * COL_MULT
    return cols ^ srl(cols, 16)


def mixed(rows, cols):
    shape = rows.shape[0], cols.shape[1]
    h = rows.reshape(shape[0] // RANK, RANK, rows.shape[1]) ^ cols[None]
    h = h.reshape(shape) * MIX_A
    h = h ^ srl(h, 13)
    return h * MIX_B


def centred_sum(h):
    h = h ^ srl(h, 16)
    s = (h & 0x00FF00FF) + (srl(h, 8) | -0xFF0100)
    return (s * 0x10001).astype(jnp.float32).astype(jnp.bfloat16)


def byte_planes(h):
    low = h.astype(jnp.int16)
    high = srl(h, 16).astype(jnp.int16)
    low = low ^ high
    eight = jnp.int16(8)
    planes = [low, high, srl(low, eight), srl(high, eight)]
    return [p.astype(jnp.uint8).astype(jnp.bfloat16) for p in planes]


COLS = 256
LANES = 128
PAIR = 2


def fill_step(step, bases, row_base, col_base, tile):
    rows = step_keys(step, bases, row_base[...])
    for c in range(0, K, COLS):
        part = centred_sum(mixed(rows, col_base[:, c:c + COLS]))
        for n in range(0, COLS, LANES):
            tile[(c + n) // LANES] = part[:, n:n + LANES]


def fill_tables(plan, first, count, refs, out):
    bases, row_base, col_base, tiles, sems = refs
    row_base[...] = row_offsets(plan)
    col_base[...] = column_keys(RANK)

    def body(n, carry):
        fill_step(n + first, bases, row_base, col_base, tiles.at[n])
        pltpu.make_async_copy(tiles.at[n], out.at[n + first], sems.at[n]).start()
        return carry

    lax.fori_loop(0, count, body, 0)

    def wait():
        for n in range(count):
            pltpu.make_async_copy(tiles.at[n], out.at[n + first], sems.at[n]).wait()

    return wait


def fill_scratch(plan, count):
    return [
        pltpu.VMEM((plan.sub, COLS), jnp.int32),
        pltpu.VMEM((RANK, K), jnp.int32),
        pltpu.VMEM((count, K // LANES, plan.sub, LANES), jnp.bfloat16),
        pltpu.SemaphoreType.DMA((count,)),
    ]


def tiles_shape(plan, total):
    return jax.ShapeDtypeStruct((total, K // LANES, plan.sub, LANES), jnp.bfloat16)


def stored_table(plan, bases, first, count, after, so_far):
    smem = pl.BlockSpec(memory_space=pltpu.SMEM)
    anywhere = pl.BlockSpec(memory_space=pl.ANY)

    def kernel(bases, after, so_far, out, *scratch):
        fill_tables(plan, first, count, (bases,) + scratch, out)()

    return pl.pallas_call(
        kernel,
        in_specs=[smem, anywhere, anywhere],
        out_specs=anywhere,
        out_shape=jax.ShapeDtypeStruct(so_far.shape, so_far.dtype),
        scratch_shapes=fill_scratch(plan, count),
        input_output_aliases={2: 0},
        name="stored_table",
    )(bases, after, so_far)


def project_kernel(plan, stored, scale, devices):
    rounds = (plan.steps - stored) // PAIR
    depth = 2 * RANK * plan.examples
    parts = 4
    slab = plan.sub // parts

    def pick(grads, step):
        rank = step % RANK
        rows = lax.broadcasted_iota(jnp.int32, (RANK, plan.sub), 0) == rank
        parts = []
        for e in range(plan.examples):
            g = jnp.where(rows, grads[e, 0], 0.0)
            top = g.astype(jnp.bfloat16).astype(jnp.float32)
            parts += [top, g - top]
        return rows_of(parts).astype(jnp.bfloat16)

    def kernel(bases, grads, old_grads, tiles, out, acc, row_base, col_base):
        i = pl.program_id(0)

        @pl.when(i == 0)
        def _():
            acc[...] = jnp.zeros_like(acc)
            row_base[...] = row_offsets(plan)
            col_base[...] = column_keys(RANK)

        old = pick(old_grads, i)
        old = jnp.where(i < stored, old.astype(jnp.float32), 0.0)
        fix = jnp.sum(old, axis=1, keepdims=True)
        old = (old * (1.0 / 65536.0)).astype(jnp.bfloat16)
        lefts, rows = [], []
        for p in range(PAIR):
            step = stored + PAIR * i + p
            rows.append(step_keys(step, bases, row_base[...]))
            left = pick(grads, step)
            fix = fix - 510.0 * jnp.sum(left.astype(jnp.float32), axis=1, keepdims=True)
            lefts.append([jnp.concatenate([left[:, b:b + slab]] * parts, axis=1) for b in range(0, plan.sub, slab)])
        for c in range(0, K, COLS):
            a = acc[:, c:c + COLS] + fix
            for p in range(PAIR):
                for n in range(parts):
                    planes = byte_planes(mixed(rows[p][n * slab:(n + 1) * slab], col_base[:, c:c + COLS]))
                    a = a + jnp.dot(lefts[p][n], rows_of(planes), preferred_element_type=jnp.float32)
            tile = jnp.concatenate([tiles[0, (c + n) // LANES] for n in range(0, COLS, LANES)], axis=1)
            a = a + jnp.dot(old, tile, preferred_element_type=jnp.float32)
            acc[:, c:c + COLS] = a

        @pl.when(i == rounds - 1)
        def _():
            width = K // devices
            for e in range(plan.examples):
                part = acc[e * 2 * RANK:(e + 1) * 2 * RANK, :]
                total = jnp.sum(part, axis=0, keepdims=True) * scale
                for d in range(devices):
                    out[d, e:e + 1, :] = total[:, d * width:(d + 1) * width]

    return kernel, depth, rounds


def project(plan, bases, grads, tiles, stored, scale, devices):
    kernel, depth, rounds = project_kernel(plan, stored, scale, devices)
    smem = pl.BlockSpec(memory_space=pltpu.SMEM)
    parts = plan.block // plan.sub

    def place(step):
        number = step // RANK
        return (0, number // parts, 0, number % parts)

    last = stored - 1
    return pl.pallas_call(
        kernel,
        grid=(rounds,),
        in_specs=[
            smem,
            pl.BlockSpec((plan.examples, 1, RANK, plan.sub), lambda i: place(PAIR * i + stored)),
            pl.BlockSpec((plan.examples, 1, RANK, plan.sub), lambda i: place(jnp.minimum(i, last))),
            pl.BlockSpec((1, K // LANES, plan.sub, LANES), lambda i: (jnp.minimum(i, last), 0, 0, 0)),
        ],
        out_specs=pl.BlockSpec((devices, plan.examples, K // devices), lambda i: (0, 0, 0)),
        out_shape=jax.ShapeDtypeStruct((devices, plan.examples, K // devices), jnp.float32),
        scratch_shapes=[
            pltpu.VMEM((depth, K), jnp.float32),
            pltpu.VMEM((plan.sub, COLS), jnp.int32),
            pltpu.VMEM((RANK, K), jnp.int32),
        ],
        name="project",
    )(bases, grads, grads, tiles)


def swap(x, axis, bit):
    size = lax.axis_size(axis)
    return lax.ppermute(x, axis, [(i, i ^ (1 << bit)) for i in range(size)])


def shards(*args):
    data = args[:9]
    factors = args[9:14]
    mask, seeds = args[14:16]
    plan = Plan(tuple(x.shape[-1] for x in data), data[0].shape[0], lax.axis_size("proj"))
    table = jnp.asarray(plan.table)
    counts = [max(1, c * plan.steps // 128) for c in STORED_STEPS][:3 + len(plan.bits)]
    counts[-1] += sum(counts) % PAIR
    starts = [sum(counts[:n]) for n in range(len(counts))]
    stored = sum(counts)
    own, tiles, bases = products(plan, data, factors, table, seeds, counts[0], stored)

    def cover(received, sent, number):
        nonlocal tiles
        tiles = stored_table(plan, bases, starts[number], counts[number], sent, tiles)
        received, tiles = lax.optimization_barrier((received, tiles))
        return received

    if lax.axis_size("mp") == 2:
        other = swap(own, "mp", 0)
    else:
        own = lax.psum(own, "mp")
        other = jnp.zeros_like(own)
    other = cover(other, own, 1)
    keep, send, tiles = gradients(
        plan, data, own, other, mask.reshape(1, -1), plan.bits[0], bases, starts[2], counts[2], tiles)
    j = lax.axis_index("proj")
    x = None
    for number, bit in enumerate(plan.bits):
        if number > 0:
            half = x.shape[0] // 2
            side = (j >> bit) & 1
            send = lax.dynamic_slice_in_dim(x, (1 - side) * half, half, 0)
            keep = lax.dynamic_slice_in_dim(x, side * half, half, 0)
        received = cover(swap(send, "proj", bit), send, number + 3)
        x = keep + received
    x = x[None]
    if plan.examples > 1:
        groups = [[e * plan.group + i for e in range(plan.examples)] for i in range(plan.group)]
        x = x.reshape((plan.examples, plan.own_blocks) + x.shape[2:])
        x = lax.all_to_all(x, "proj", 0, 0, axis_index_groups=groups, tiled=True)
    scale = 1.0 / (LENGTH * math.sqrt(21845.0 * K))
    devices = lax.axis_size("mp") * plan.owners
    pieces = project(plan, bases, x, tiles, stored, scale, devices)
    got = lax.all_to_all(pieces, ("mp", "proj"), 0, 0, tiled=True)
    return got.sum(axis=0)


def solution(mesh):
    in_specs = (
        P("proj", "mp"),
        P("proj", "mp"),
        P("proj", "mp"),
        P("proj", "mp"),
        P("proj", "mp"),
        P("proj", None, "mp"),
        P("proj", "mp"),
        P("proj", None, "mp"),
        P("proj", "mp"),
        P(None, None, "mp"),
        P(None, "mp"),
        P(None, None, "mp"),
        P(None, None, "mp"),
        P(None, None, "mp"),
        P("proj"),
        P(),
    )
    out_specs = P(None, ("mp", "proj"))
    return jax.shard_map(shards, mesh=mesh, in_specs=in_specs, out_specs=out_specs, check_vma=False)
```

```python
import math

import jax
import jax.numpy as jnp
import numpy as np
from jax import lax
from jax.experimental import pallas as pl
from jax.experimental.pallas import tpu as pltpu
from jax.sharding import PartitionSpec as P

K = 2048
LENGTH = 2048
RANK = 8
ROWS = 256
SEED_MULT = 1103515245
ROW_MULT = 668265263
COL_MULT = -1640531535
MIX_A = -2048144789
MIX_B = -1028477387
STORED_STEPS = (6, 2, 5, 5, 11, 13)

srl = lax.shift_right_logical


def chunk_of(width, unit, limit=4608):
    for parts in range(1, width // unit + 1):
        if width % (parts * unit) == 0 and width // parts <= limit:
            return width // parts
    return width


def wrapped(number):
    return (number + 2**31) % 2**32 - 2**31


def rows_of(parts):
    return jnp.concatenate(parts, axis=0) if len(parts) > 1 else parts[0]


class Plan:
    def __init__(self, widths, tokens, owners):
        self.widths = widths
        self.tokens = tokens
        self.owners = owners
        hid, att, gin, dwn, qry, kvw, aow, guw, dow = widths
        self.pieces = [
            (0, (24, 32, 40), (0, 2, 4), hid),
            (4, (0,), (1,), qry),
            (5, (8, 16), (3, 5), kvw),
            (1, (56,), (6,), att),
            (6, (48,), (7,), aow),
            (2, (80, 88), (8, 10), gin),
            (7, (64, 72), (9, 11), guw),
            (3, (104,), (12,), dwn),
            (8, (96,), (13,), dow),
        ]
        self.block = 0
        for _, _, _, width in self.pieces:
            self.block = math.gcd(self.block, width)
        while self.block > 512:
            self.block //= 2
        seg_tab, off_tab, width_tab = [], [], []
        self.first_block = {}
        for _, _, segs, width in self.pieces:
            for seg in segs:
                self.first_block[seg] = len(seg_tab)
                for number in range(width // self.block):
                    seg_tab.append(seg)
                    off_tab.append(number * self.block)
                    width_tab.append(width)
        self.blocks = len(seg_tab)
        self.table = np.array([seg_tab, off_tab, width_tab], np.int32)
        self.group = LENGTH // tokens
        self.examples = owners // self.group
        self.own_blocks = self.blocks // owners
        self.sub = min(ROWS, self.block)
        self.steps = self.own_blocks * (self.block // self.sub) * RANK
        bits = self.group.bit_length() - 1
        self.bits = ([0, 1] + list(reversed(range(2, bits))))[:bits]

    def first_own(self):
        j = lax.axis_index("proj")
        piece = 0
        for bit in self.bits:
            piece = piece * 2 + ((j >> bit) & 1)
        return piece * (self.blocks // self.group) + (j // self.group) * self.own_blocks


def every_other(x, first):
    wide = x.shape[1]
    u = lax.broadcasted_iota(jnp.int32, (wide, wide // 2), 0)
    t = lax.broadcasted_iota(jnp.int32, (wide, wide // 2), 1)
    choose = (u == 2 * t + first).astype(jnp.float32).astype(jnp.bfloat16)
    total = None
    for _ in range(3):
        term = x.astype(jnp.bfloat16)
        x = x - term.astype(jnp.float32)
        got = jnp.dot(term, choose, preferred_element_type=jnp.float32)
        total = got if total is None else total + got
    return total


NARROW = (0, 4, 1, 6, 2, 8)
NARROW_ROWS = ((0, 24), (24, 8), (48, 8), (56, 8), (64, 16), (104, 8))


def product_kernel(plan, count):
    wide = plan.widths[3]
    part = chunk_of(wide, plan.block, PART)
    trips = wide // part

    def kernel(*refs):
        data = refs[:9]
        aif, daf, aof, kvb, gub = refs[9:14]
        table, seeds = refs[14:16]
        out, tiles, bases = refs[16:19]
        narrow, kv, gate_up, down, narrow_sems, wide_sems = refs[19:25]
        narrow_fac, kv_fac, gate_up_fac, down_fac, fac_sems = refs[25:30]
        fill_refs = (bases,) + refs[30:]
        pairs = [(aif.at[0], narrow_fac.at[0, pl.ds(0, RANK)]), (aif.at[1], narrow_fac.at[0, pl.ds(RANK, RANK)]),
                 (aif.at[2], narrow_fac.at[0, pl.ds(2 * RANK, RANK)]), (aof.at[0], narrow_fac.at[1, pl.ds(0, RANK)]),
                 (aif.at[3], narrow_fac.at[2, pl.ds(0, RANK)]), (aof.at[1], narrow_fac.at[3, pl.ds(0, RANK)]),
                 (aif.at[4], narrow_fac.at[4, pl.ds(0, RANK)]), (aif.at[5], narrow_fac.at[4, pl.ds(RANK, RANK)]),
                 (aof.at[2], narrow_fac.at[5, pl.ds(0, RANK)]), (daf, down_fac)]
        pairs += [(kvb.at[i], kv_fac.at[pl.ds(i * RANK, RANK)]) for i in range(2)]
        pairs += [(gub.at[i], gate_up_fac.at[pl.ds(i * RANK, RANK)]) for i in range(2)]
        loads = [pltpu.make_async_copy(x, y, fac_sems.at[n]) for n, (x, y) in enumerate(pairs)]
        loads += [pltpu.make_async_copy(data[arg], narrow.at[n], narrow_sems.at[n]) for n, arg in enumerate(NARROW)]
        loads.append(pltpu.make_async_copy(data[5], kv, narrow_sems.at[len(NARROW)]))

        def wide_copies(j):
            cols = pl.ds(pl.multiple_of(j * part, LANES), part)
            return [
                pltpu.make_async_copy(data[7].at[:, :, cols], gate_up.at[:, :, cols], wide_sems.at[0, j]),
                pltpu.make_async_copy(data[3].at[:, cols], down.at[:, cols], wide_sems.at[1, j]),
            ]

        for load in loads:
            load.start()

        def begin(j, carry):
            for copy in wide_copies(j):
                copy.start()
            return carry

        lax.fori_loop(0, trips, begin, 0)
        block = plan.first_own()
        for n in range(plan.steps // RANK):
            parts = plan.block // plan.sub
            seg = table[0, block + n // parts]
            feature = lax.axis_index("mp") * table[2, block + n // parts] + table[1, block + n // parts]
            feature = feature + (n % parts) * plan.sub
            bases[n] = seeds[seg] * SEED_MULT + feature * wrapped(RANK * ROW_MULT)

        def contract(left, right):
            return lax.dot_general(left, right, (((1,), (1,)), ((), ())), preferred_element_type=jnp.float32)

        def wide_part(j, carry):
            for copy in wide_copies(j):
                copy.wait()
            cols = pl.ds(pl.multiple_of(j * part, LANES), part)
            both = gate_up[:, :, cols].reshape(2 * plan.tokens, part)
            return carry[0] + contract(gate_up_fac[:, cols], both), carry[1] + contract(down_fac[:, cols], down[:, cols])

        zero = jnp.zeros((2 * RANK, 2 * plan.tokens), jnp.float32), jnp.zeros((RANK, plan.tokens), jnp.float32)
        finish = fill_tables(plan, 0, count, fill_refs, tiles)
        for load in loads:
            load.wait()

        def narrow_part(n, carry):
            sums[n] = contract(narrow_fac[n], narrow[n])
            return carry

        sums = refs[-1]
        lax.fori_loop(0, len(NARROW), narrow_part, 0)
        for n, (place, rows) in enumerate(NARROW_ROWS):
            out[place:place + rows, :] = sums[n, 0:rows]
        kv_sum = contract(kv_fac[...], kv[...].reshape(2 * plan.tokens, plan.widths[5]))
        gate_up_sum, down_sum = lax.fori_loop(0, trips, wide_part, zero)
        out[96:104, :] = down_sum
        for i in range(2):
            out[32 + i * RANK:32 + (i + 1) * RANK, :] = every_other(kv_sum[i * RANK:(i + 1) * RANK], i)
            out[80 + i * RANK:80 + (i + 1) * RANK, :] = every_other(gate_up_sum[i * RANK:(i + 1) * RANK], i)
        finish()

    return kernel


def copy_count(plan):
    return sum(width // chunk_of(width, plan.block) for width in plan.widths)


def data_buffers(plan, data):
    return [pltpu.VMEM(x.shape, jnp.bfloat16) for x in data]


def products(plan, data, factors, table, seeds, count, total):
    anywhere = pl.BlockSpec(memory_space=pl.ANY)
    smem = pl.BlockSpec(memory_space=pltpu.SMEM)
    whole = pl.BlockSpec(memory_space=pltpu.VMEM)
    return pl.pallas_call(
        product_kernel(plan, count),
        in_specs=[anywhere] * 14 + [smem, smem],
        out_specs=[whole, anywhere, smem],
        out_shape=[
            jax.ShapeDtypeStruct((14 * RANK, plan.tokens), jnp.float32),
            tiles_shape(plan, total),
            jax.ShapeDtypeStruct((plan.steps // RANK,), jnp.int32),
        ],
        scratch_shapes=[
            pltpu.VMEM((len(NARROW),) + data[0].shape, jnp.bfloat16),
            pltpu.VMEM(data[5].shape, jnp.bfloat16),
            pltpu.VMEM(data[7].shape, jnp.bfloat16),
            pltpu.VMEM(data[3].shape, jnp.bfloat16),
            pltpu.SemaphoreType.DMA((len(NARROW) + 1,)),
            pltpu.SemaphoreType.DMA((2, plan.widths[3] // chunk_of(plan.widths[3], plan.block, PART))),
            pltpu.VMEM((len(NARROW), 3 * RANK, plan.widths[0]), jnp.bfloat16),
            pltpu.VMEM((2 * RANK, plan.widths[5]), jnp.bfloat16),
            pltpu.VMEM((2 * RANK, plan.widths[7]), jnp.bfloat16),
            pltpu.VMEM((RANK, plan.widths[3]), jnp.bfloat16),
            pltpu.SemaphoreType.DMA((14,)),
        ]
        + fill_scratch(plan, count)
        + [pltpu.VMEM((len(NARROW), 3 * RANK, plan.tokens), jnp.float32)],
        name="products",
    )(*data, *factors, table, seeds)


def gradient_kernel(plan, split, first, count):
    def kernel(*refs):
        data = refs[:9]
        own, other, mask = refs[9:12]
        bases = refs[12]
        keep, send, tiles = refs[14:17]
        bufs = refs[17:26]
        grads, sems, out_sems = refs[26:29]
        fill_refs = (bases,) + refs[29:]
        copies = {}
        number = 0
        for arg, _, _, width in plan.pieces:
            step = chunk_of(width, plan.block)
            for start in range(0, width, step):
                view = (slice(None),) * (len(data[arg].shape) - 1) + (pl.ds(start, step),)
                copies[arg, start] = pltpu.make_async_copy(data[arg].at[view], bufs[arg].at[view], sems.at[number])
                number += 1
        for copy in copies.values():
            copy.start()
        finish = fill_tables(plan, first, count, fill_refs, tiles)
        total = own[...] + other[...]
        turned = total * mask[...].astype(jnp.float32)
        tokens = plan.tokens
        half = plan.blocks // 2
        for arg, places, segs, width in plan.pieces:
            left = rows_of([turned[p:p + RANK] for p in places]).astype(jnp.bfloat16)
            if len(data[arg].shape) == 3:
                t = lax.broadcasted_iota(jnp.int32, (tokens, 2 * tokens), 0)
                u = lax.broadcasted_iota(jnp.int32, (tokens, 2 * tokens), 1)
                parts = []
                for i in range(2):
                    spread = (u == 2 * t + i).astype(jnp.float32).astype(jnp.bfloat16)
                    one = turned[places[i]:places[i] + RANK].astype(jnp.bfloat16)
                    parts.append(jnp.dot(one, spread, preferred_element_type=jnp.float32))
                left = rows_of(parts).astype(jnp.bfloat16)
            step = chunk_of(width, plan.block)
            for start in range(0, width, step):
                copies[arg, start].wait()
                cols = pl.ds(start, step)
                if len(data[arg].shape) == 3:
                    right = bufs[arg][:, :, cols].reshape(2 * tokens, step)
                else:
                    right = bufs[arg][:, cols]
                got = jnp.dot(left, right, preferred_element_type=jnp.float32)
                for i, seg in enumerate(segs):
                    for k in range(step // plan.block):
                        block = plan.first_block[seg] + start // plan.block + k
                        grads[block // half, block % half] = got[
                            i * RANK:(i + 1) * RANK, k * plan.block:(k + 1) * plan.block]
        bit = (lax.axis_index("proj") >> split) & 1
        sent = pltpu.make_async_copy(grads.at[1 - bit], send, out_sems.at[0])
        kept = pltpu.make_async_copy(grads.at[bit], keep, out_sems.at[1])
        sent.start()
        kept.start()
        finish()
        sent.wait()
        kept.wait()

    return kernel


def gradients(plan, data, own, other, mask, split, bases, first, count, so_far):
    anywhere = pl.BlockSpec(memory_space=pl.ANY)
    smem = pl.BlockSpec(memory_space=pltpu.SMEM)
    whole = pl.BlockSpec(memory_space=pltpu.VMEM)
    half = jax.ShapeDtypeStruct((plan.blocks // 2, RANK, plan.block), jnp.float32)
    return pl.pallas_call(
        gradient_kernel(plan, split, first, count),
        in_specs=[anywhere] * 9 + [whole] * 3 + [smem, anywhere],
        out_specs=[anywhere] * 3,
        out_shape=[half, half, jax.ShapeDtypeStruct(so_far.shape, so_far.dtype)],
        scratch_shapes=data_buffers(plan, data)
        + [
            pltpu.VMEM((2, plan.blocks // 2, RANK, plan.block), jnp.float32),
            pltpu.SemaphoreType.DMA((copy_count(plan),)),
            pltpu.SemaphoreType.DMA((2,)),
        ]
        + fill_scratch(plan, count),
        input_output_aliases={13: 2},
        name="gradients",
    )(*data, own, other, mask, bases, so_far)


def row_offsets(plan):
    return lax.broadcasted_iota(jnp.int32, (plan.sub, LANES), 0) * wrapped(RANK * ROW_MULT)


def step_keys(step, bases, offsets):
    turn = wrapped(step % RANK * ROW_MULT) if isinstance(step, int) else (step % RANK) * ROW_MULT
    key = bases[step // RANK] + turn + offsets
    key = key ^ srl(key, 16)
    return jnp.concatenate([key] * (COLS // LANES), axis=1)


def column_keys(copies=1):
    cols = lax.broadcasted_iota(jnp.int32, (copies, K), 1) * COL_MULT
    return cols ^ srl(cols, 16)


def mixed(rows, cols):
    shape = rows.shape[0], cols.shape[1]
    h = rows.reshape(shape[0] // RANK, RANK, rows.shape[1]) ^ cols[None]
    h = h.reshape(shape) * MIX_A
    h = h ^ srl(h, 13)
    return h * MIX_B


def centred_sum(h):
    h = h ^ srl(h, 16)
    s = (h & 0x00FF00FF) + (srl(h, 8) | -0xFF0100)
    return (s * 0x10001).astype(jnp.float32).astype(jnp.bfloat16)


def byte_planes(h):
    low = h.astype(jnp.int16)
    high = srl(h, 16).astype(jnp.int16)
    low = low ^ high
    eight = jnp.int16(8)
    planes = [low, high, srl(low, eight), srl(high, eight)]
    return [p.astype(jnp.uint8).astype(jnp.bfloat16) for p in planes]


COLS = 256
LANES = 128
PAIR = 2
PART = 1536


def fill_step(step, bases, row_base, col_base, tile):
    rows = step_keys(step, bases, row_base[...])
    for c in range(0, K, COLS):
        part = centred_sum(mixed(rows, col_base[:, c:c + COLS]))
        for n in range(0, COLS, LANES):
            tile[(c + n) // LANES] = part[:, n:n + LANES]


def fill_tables(plan, first, count, refs, out):
    bases, row_base, col_base, tiles, sems = refs[:5]
    row_base[...] = row_offsets(plan)
    col_base[...] = column_keys(RANK)

    def body(n, carry):
        fill_step(n + first, bases, row_base, col_base, tiles.at[n])
        pltpu.make_async_copy(tiles.at[n], out.at[n + first], sems.at[n]).start()
        return carry

    lax.fori_loop(0, count, body, 0)

    def wait():
        for n in range(count):
            pltpu.make_async_copy(tiles.at[n], out.at[n + first], sems.at[n]).wait()

    return wait


def fill_scratch(plan, count):
    return [
        pltpu.VMEM((plan.sub, LANES), jnp.int32),
        pltpu.VMEM((RANK, K), jnp.int32),
        pltpu.VMEM((count, K // LANES, plan.sub, LANES), jnp.bfloat16),
        pltpu.SemaphoreType.DMA((count,)),
    ]


def tiles_shape(plan, total):
    return jax.ShapeDtypeStruct((total, K // LANES, plan.sub, LANES), jnp.bfloat16)


def stored_table(plan, bases, first, count, after, so_far):
    smem = pl.BlockSpec(memory_space=pltpu.SMEM)
    anywhere = pl.BlockSpec(memory_space=pl.ANY)

    def kernel(bases, after, so_far, out, *scratch):
        fill_tables(plan, first, count, (bases,) + scratch, out)()

    return pl.pallas_call(
        kernel,
        in_specs=[smem, anywhere, anywhere],
        out_specs=anywhere,
        out_shape=jax.ShapeDtypeStruct(so_far.shape, so_far.dtype),
        scratch_shapes=fill_scratch(plan, count),
        input_output_aliases={2: 0},
        name="stored_table",
    )(bases, after, so_far)


def project_kernel(plan, stored, scale, devices):
    rounds = (plan.steps - stored) // PAIR
    depth = 2 * RANK * plan.examples
    parts = 4
    slab = plan.sub // parts

    def pick(grads, step):
        rank = step % RANK
        rows = lax.broadcasted_iota(jnp.int32, (RANK, plan.sub), 0) == rank
        parts = []
        for e in range(plan.examples):
            g = jnp.where(rows, grads[e, 0], 0.0)
            top = g.astype(jnp.bfloat16).astype(jnp.float32)
            parts += [top, g - top]
        return rows_of(parts).astype(jnp.bfloat16)

    def kernel(bases, grads, old_grads, tiles, out, acc, row_base, col_base):
        i = pl.program_id(0)

        @pl.when(i == 0)
        def _():
            acc[...] = jnp.zeros_like(acc)
            row_base[...] = row_offsets(plan)
            col_base[...] = column_keys(RANK)

        old = pick(old_grads, i)
        old = jnp.where(i < stored, old.astype(jnp.float32), 0.0)
        fix = jnp.sum(old, axis=1, keepdims=True)
        old = (old * (1.0 / 65536.0)).astype(jnp.bfloat16)
        lefts, rows = [], []
        for p in range(PAIR):
            step = stored + PAIR * i + p
            rows.append(step_keys(step, bases, row_base[...]))
            left = pick(grads, step)
            fix = fix - 510.0 * jnp.sum(left.astype(jnp.float32), axis=1, keepdims=True)
            lefts.append([jnp.concatenate([left[:, b:b + slab]] * parts, axis=1) for b in range(0, plan.sub, slab)])
        for c in range(0, K, COLS):
            a = acc[:, c:c + COLS] + fix
            for p in range(PAIR):
                for n in range(parts):
                    planes = byte_planes(mixed(rows[p][n * slab:(n + 1) * slab], col_base[:, c:c + COLS]))
                    a = a + jnp.dot(lefts[p][n], rows_of(planes), preferred_element_type=jnp.float32)
            tile = jnp.concatenate([tiles[0, (c + n) // LANES] for n in range(0, COLS, LANES)], axis=1)
            a = a + jnp.dot(old, tile, preferred_element_type=jnp.float32)
            acc[:, c:c + COLS] = a

        @pl.when(i == rounds - 1)
        def _():
            width = K // devices
            for e in range(plan.examples):
                part = acc[e * 2 * RANK:(e + 1) * 2 * RANK, :]
                total = jnp.sum(part, axis=0, keepdims=True) * scale
                for d in range(devices):
                    out[d, e:e + 1, :] = total[:, d * width:(d + 1) * width]

    return kernel, depth, rounds


def project(plan, bases, grads, tiles, stored, scale, devices):
    kernel, depth, rounds = project_kernel(plan, stored, scale, devices)
    smem = pl.BlockSpec(memory_space=pltpu.SMEM)
    parts = plan.block // plan.sub

    def place(step):
        number = step // RANK
        return (0, number // parts, 0, number % parts)

    last = stored - 1
    return pl.pallas_call(
        kernel,
        grid=(rounds,),
        in_specs=[
            smem,
            pl.BlockSpec((plan.examples, 1, RANK, plan.sub), lambda i: place(PAIR * i + stored)),
            pl.BlockSpec((plan.examples, 1, RANK, plan.sub), lambda i: place(jnp.minimum(i, last))),
            pl.BlockSpec((1, K // LANES, plan.sub, LANES), lambda i: (jnp.minimum(i, last), 0, 0, 0)),
        ],
        out_specs=pl.BlockSpec((devices, plan.examples, K // devices), lambda i: (0, 0, 0)),
        out_shape=jax.ShapeDtypeStruct((devices, plan.examples, K // devices), jnp.float32),
        scratch_shapes=[
            pltpu.VMEM((depth, K), jnp.float32),
            pltpu.VMEM((plan.sub, LANES), jnp.int32),
            pltpu.VMEM((RANK, K), jnp.int32),
        ],
        name="project",
    )(bases, grads, grads, tiles)


def swap(x, axis, bit):
    size = lax.axis_size(axis)
    return lax.ppermute(x, axis, [(i, i ^ (1 << bit)) for i in range(size)])


def shards(*args):
    data = args[:9]
    factors = args[9:14]
    mask, seeds = args[14:16]
    plan = Plan(tuple(x.shape[-1] for x in data), data[0].shape[0], lax.axis_size("proj"))
    table = jnp.asarray(plan.table)
    counts = [max(1, c * plan.steps // 128) for c in STORED_STEPS][:6]
    counts[-1] += sum(counts) % PAIR
    starts = [sum(counts[:n]) for n in range(len(counts))]
    stored = sum(counts)
    own, tiles, bases = products(plan, data, factors, table, seeds, counts[0], stored)

    def cover(received, sent, number):
        nonlocal tiles
        tiles = stored_table(plan, bases, starts[number], counts[number], sent, tiles)
        received, tiles = lax.optimization_barrier((received, tiles))
        return received

    if lax.axis_size("mp") == 2:
        other = swap(own, "mp", 0)
    else:
        own = lax.psum(own, "mp")
        other = jnp.zeros_like(own)
    other = cover(other, own, 1)
    keep, send, tiles = gradients(
        plan, data, own, other, mask.reshape(1, -1), plan.bits[0], bases, starts[2], counts[2], tiles)
    j = lax.axis_index("proj")
    low = len(plan.bits[:2])
    x = None
    for number, bit in enumerate(plan.bits[:2]):
        if number > 0:
            half = x.shape[0] // 2
            side = (j >> bit) & 1
            send = lax.dynamic_slice_in_dim(x, (1 - side) * half, half, 0)
            keep = lax.dynamic_slice_in_dim(x, side * half, half, 0)
        received = cover(swap(send, "proj", bit), send, number + 3)
        x = keep + received
    ways = plan.group >> low
    if ways > 1:
        size = x.shape[0] // ways
        place = (j >> low) % ways
        sends = [lax.dynamic_slice_in_dim(x, (place ^ d) * size, size, 0) for d in range(ways)]
        got = [lax.ppermute(sends[d], "proj", [(i, i ^ (d << low)) for i in range(plan.owners)]) for d in range(1, ways)]
        got = cover(got, sends[0], low + 3)
        x = sends[0]
        for one in got:
            x = x + one
    x = x[None]
    if plan.examples > 1:
        groups = [[e * plan.group + i for e in range(plan.examples)] for i in range(plan.group)]
        x = x.reshape((plan.examples, plan.own_blocks) + x.shape[2:])
        x = lax.all_to_all(x, "proj", 0, 0, axis_index_groups=groups, tiled=True)
    scale = 1.0 / (LENGTH * math.sqrt(21845.0 * K))
    devices = lax.axis_size("mp") * plan.owners
    pieces = project(plan, bases, x, tiles, stored, scale, devices)
    got = lax.all_to_all(pieces, ("mp", "proj"), 0, 0, tiled=True)
    return got.sum(axis=0)


def solution(mesh):
    in_specs = (
        P("proj", "mp"),
        P("proj", "mp"),
        P("proj", "mp"),
        P("proj", "mp"),
        P("proj", "mp"),
        P("proj", None, "mp"),
        P("proj", "mp"),
        P("proj", None, "mp"),
        P("proj", "mp"),
        P(None, None, "mp"),
        P(None, "mp"),
        P(None, None, "mp"),
        P(None, None, "mp"),
        P(None, None, "mp"),
        P("proj"),
        P(),
    )
    out_specs = P(None, ("mp", "proj"))
    return jax.shard_map(shards, mesh=mesh, in_specs=in_specs, out_specs=out_specs, check_vma=False)
```

```python
import math

import jax
import jax.numpy as jnp
import numpy as np
from jax import lax
from jax.experimental import pallas as pl
from jax.experimental.pallas import tpu as pltpu
from jax.sharding import PartitionSpec as P

K = 2048
LENGTH = 2048
RANK = 8
ROWS = 256
SEED_MULT = 1103515245
ROW_MULT = 668265263
COL_MULT = -1640531535
MIX_A = -2048144789
MIX_B = -1028477387
STORED_STEPS = (6, 2, 5, 5, 11, 13)

srl = lax.shift_right_logical


def chunk_of(width, unit, limit=4608):
    for parts in range(1, width // unit + 1):
        if width % (parts * unit) == 0 and width // parts <= limit:
            return width // parts
    return width


def wrapped(number):
    return (number + 2**31) % 2**32 - 2**31


def rows_of(parts):
    return jnp.concatenate(parts, axis=0) if len(parts) > 1 else parts[0]


class Plan:
    def __init__(self, widths, tokens, owners):
        self.widths = widths
        self.tokens = tokens
        self.owners = owners
        hid, att, gin, dwn, qry, kvw, aow, guw, dow = widths
        self.pieces = [
            (0, (24, 32, 40), (0, 2, 4), hid),
            (4, (0,), (1,), qry),
            (5, (8, 16), (3, 5), kvw),
            (1, (56,), (6,), att),
            (6, (48,), (7,), aow),
            (2, (80, 88), (8, 10), gin),
            (7, (64, 72), (9, 11), guw),
            (3, (104,), (12,), dwn),
            (8, (96,), (13,), dow),
        ]
        self.block = 0
        for _, _, _, width in self.pieces:
            self.block = math.gcd(self.block, width)
        while self.block > 512:
            self.block //= 2
        seg_tab, off_tab, width_tab = [], [], []
        self.first_block = {}
        for _, _, segs, width in self.pieces:
            for seg in segs:
                self.first_block[seg] = len(seg_tab)
                for number in range(width // self.block):
                    seg_tab.append(seg)
                    off_tab.append(number * self.block)
                    width_tab.append(width)
        self.blocks = len(seg_tab)
        self.table = np.array([seg_tab, off_tab, width_tab], np.int32)
        self.group = LENGTH // tokens
        self.examples = owners // self.group
        self.own_blocks = self.blocks // owners
        self.sub = min(ROWS, self.block)
        self.steps = self.own_blocks * (self.block // self.sub) * RANK
        bits = self.group.bit_length() - 1
        self.bits = ([0, 1] + list(reversed(range(2, bits))))[:bits]

    def first_own(self):
        j = lax.axis_index("proj")
        piece = 0
        for bit in self.bits:
            piece = piece * 2 + ((j >> bit) & 1)
        return piece * (self.blocks // self.group) + (j // self.group) * self.own_blocks


def every_other(x, first):
    wide = x.shape[1]
    u = lax.broadcasted_iota(jnp.int32, (wide, wide // 2), 0)
    t = lax.broadcasted_iota(jnp.int32, (wide, wide // 2), 1)
    choose = (u == 2 * t + first).astype(jnp.float32).astype(jnp.bfloat16)
    total = None
    for _ in range(3):
        term = x.astype(jnp.bfloat16)
        x = x - term.astype(jnp.float32)
        got = jnp.dot(term, choose, preferred_element_type=jnp.float32)
        total = got if total is None else total + got
    return total


NARROW = (0, 4, 1, 6, 2, 8)
NARROW_ROWS = ((0, 24), (24, 8), (48, 8), (56, 8), (64, 16), (104, 8))


def product_kernel(plan, count):
    wide = plan.widths[3]
    part = chunk_of(wide, plan.block, PART)
    trips = wide // part

    def kernel(*refs):
        data = refs[:9]
        aif, daf, aof, kvb, gub = refs[9:14]
        table, seeds = refs[14:16]
        out, tiles, bases = refs[16:19]
        narrow, kv, gate_up, down, narrow_sems, wide_sems = refs[19:25]
        narrow_fac, kv_fac, gate_up_fac, down_fac, fac_sems = refs[25:30]
        fill_refs = (bases,) + refs[30:]
        pairs = [(aif.at[0], narrow_fac.at[0, pl.ds(0, RANK)]), (aif.at[1], narrow_fac.at[0, pl.ds(RANK, RANK)]),
                 (aif.at[2], narrow_fac.at[0, pl.ds(2 * RANK, RANK)]), (aof.at[0], narrow_fac.at[1, pl.ds(0, RANK)]),
                 (aif.at[3], narrow_fac.at[2, pl.ds(0, RANK)]), (aof.at[1], narrow_fac.at[3, pl.ds(0, RANK)]),
                 (aif.at[4], narrow_fac.at[4, pl.ds(0, RANK)]), (aif.at[5], narrow_fac.at[4, pl.ds(RANK, RANK)]),
                 (aof.at[2], narrow_fac.at[5, pl.ds(0, RANK)]), (daf, down_fac)]
        pairs += [(kvb.at[i], kv_fac.at[pl.ds(i * RANK, RANK)]) for i in range(2)]
        pairs += [(gub.at[i], gate_up_fac.at[pl.ds(i * RANK, RANK)]) for i in range(2)]
        loads = [pltpu.make_async_copy(x, y, fac_sems.at[n]) for n, (x, y) in enumerate(pairs)]
        loads += [pltpu.make_async_copy(data[arg], narrow.at[n], narrow_sems.at[n]) for n, arg in enumerate(NARROW)]
        loads.append(pltpu.make_async_copy(data[5], kv, narrow_sems.at[len(NARROW)]))

        def wide_copies(j):
            cols = pl.ds(pl.multiple_of(j * part, LANES), part)
            return [
                pltpu.make_async_copy(data[7].at[:, :, cols], gate_up.at[:, :, cols], wide_sems.at[0, j]),
                pltpu.make_async_copy(data[3].at[:, cols], down.at[:, cols], wide_sems.at[1, j]),
            ]

        for load in loads:
            load.start()

        def begin(j, carry):
            for copy in wide_copies(j):
                copy.start()
            return carry

        lax.fori_loop(0, trips, begin, 0)
        block = plan.first_own()
        for n in range(plan.steps // RANK):
            parts = plan.block // plan.sub
            seg = table[0, block + n // parts]
            feature = lax.axis_index("mp") * table[2, block + n // parts] + table[1, block + n // parts]
            feature = feature + (n % parts) * plan.sub
            bases[n] = seeds[seg] * SEED_MULT + feature * wrapped(RANK * ROW_MULT)

        def contract(left, right):
            return lax.dot_general(left, right, (((1,), (1,)), ((), ())), preferred_element_type=jnp.float32)

        def wide_part(j, carry):
            for copy in wide_copies(j):
                copy.wait()
            cols = pl.ds(pl.multiple_of(j * part, LANES), part)
            both = gate_up[:, :, cols].reshape(2 * plan.tokens, part)
            return carry[0] + contract(gate_up_fac[:, cols], both), carry[1] + contract(down_fac[:, cols], down[:, cols])

        zero = jnp.zeros((2 * RANK, 2 * plan.tokens), jnp.float32), jnp.zeros((RANK, plan.tokens), jnp.float32)
        finish = fill_tables(plan, 0, count, fill_refs, tiles)
        for load in loads:
            load.wait()

        def narrow_part(n, carry):
            sums[n] = contract(narrow_fac[n], narrow[n])
            return carry

        sums = refs[-1]
        lax.fori_loop(0, len(NARROW), narrow_part, 0)
        for n, (place, rows) in enumerate(NARROW_ROWS):
            out[place:place + rows, :] = sums[n, 0:rows]
        kv_sum = contract(kv_fac[...], kv[...].reshape(2 * plan.tokens, plan.widths[5]))
        gate_up_sum, down_sum = lax.fori_loop(0, trips, wide_part, zero)
        out[96:104, :] = down_sum
        for i in range(2):
            out[32 + i * RANK:32 + (i + 1) * RANK, :] = every_other(kv_sum[i * RANK:(i + 1) * RANK], i)
            out[80 + i * RANK:80 + (i + 1) * RANK, :] = every_other(gate_up_sum[i * RANK:(i + 1) * RANK], i)
        finish()

    return kernel


def copy_count(plan):
    return sum(width // chunk_of(width, plan.block) for width in plan.widths)


def data_buffers(plan, data):
    return [pltpu.VMEM(x.shape, jnp.bfloat16) for x in data]


def products(plan, data, factors, table, seeds, count, total):
    anywhere = pl.BlockSpec(memory_space=pl.ANY)
    smem = pl.BlockSpec(memory_space=pltpu.SMEM)
    whole = pl.BlockSpec(memory_space=pltpu.VMEM)
    return pl.pallas_call(
        product_kernel(plan, count),
        in_specs=[anywhere] * 14 + [smem, smem],
        out_specs=[whole, anywhere, smem],
        out_shape=[
            jax.ShapeDtypeStruct((14 * RANK, plan.tokens), jnp.float32),
            tiles_shape(plan, total),
            jax.ShapeDtypeStruct((plan.steps // RANK,), jnp.int32),
        ],
        scratch_shapes=[
            pltpu.VMEM((len(NARROW),) + data[0].shape, jnp.bfloat16),
            pltpu.VMEM(data[5].shape, jnp.bfloat16),
            pltpu.VMEM(data[7].shape, jnp.bfloat16),
            pltpu.VMEM(data[3].shape, jnp.bfloat16),
            pltpu.SemaphoreType.DMA((len(NARROW) + 1,)),
            pltpu.SemaphoreType.DMA((2, plan.widths[3] // chunk_of(plan.widths[3], plan.block, PART))),
            pltpu.VMEM((len(NARROW), 3 * RANK, plan.widths[0]), jnp.bfloat16),
            pltpu.VMEM((2 * RANK, plan.widths[5]), jnp.bfloat16),
            pltpu.VMEM((2 * RANK, plan.widths[7]), jnp.bfloat16),
            pltpu.VMEM((RANK, plan.widths[3]), jnp.bfloat16),
            pltpu.SemaphoreType.DMA((14,)),
        ]
        + fill_scratch(plan, count)
        + [pltpu.VMEM((len(NARROW), 3 * RANK, plan.tokens), jnp.float32)],
        name="products",
    )(*data, *factors, table, seeds)


def gradient_kernel(plan, split, first, count):
    def kernel(*refs):
        data = refs[:9]
        own, other, mask = refs[9:12]
        bases = refs[12]
        keep, send, tiles = refs[14:17]
        bufs = refs[17:26]
        grads, sems, out_sems = refs[26:29]
        fill_refs = (bases,) + refs[29:]
        copies = {}
        numbers = {}
        number = 0
        for arg, _, _, width in plan.pieces:
            step = chunk_of(width, plan.block)
            for start in range(0, width, step):
                view = (slice(None),) * (len(data[arg].shape) - 1) + (pl.ds(start, step),)
                numbers[arg, start] = number
                copies[arg, start] = pltpu.make_async_copy(data[arg].at[view], bufs[arg].at[view], sems.at[number])
                number += 1
        for copy in copies.values():
            copy.start()
        finish = fill_tables(plan, first, count, fill_refs, tiles)
        total = own[...] + other[...]
        turned = total * mask[...].astype(jnp.float32)
        tokens = plan.tokens
        half = plan.blocks // 2
        def left_of(arg, places):
            left = rows_of([turned[p:p + RANK] for p in places]).astype(jnp.bfloat16)
            if len(data[arg].shape) == 3:
                t = lax.broadcasted_iota(jnp.int32, (tokens, 2 * tokens), 0)
                u = lax.broadcasted_iota(jnp.int32, (tokens, 2 * tokens), 1)
                parts = []
                for i in range(2):
                    spread = (u == 2 * t + i).astype(jnp.float32).astype(jnp.bfloat16)
                    one = turned[places[i]:places[i] + RANK].astype(jnp.bfloat16)
                    parts.append(jnp.dot(one, spread, preferred_element_type=jnp.float32))
                left = rows_of(parts).astype(jnp.bfloat16)
            return left

        def one_part(arg, left, segs, start, step, copy):
            copy.wait()
            cols = pl.ds(start, step)
            if len(data[arg].shape) == 3:
                right = bufs[arg][:, :, cols].reshape(2 * tokens, step)
            else:
                right = bufs[arg][:, cols]
            got = jnp.dot(left, right, preferred_element_type=jnp.float32)
            for i, seg in enumerate(segs):
                for k in range(step // plan.block):
                    grads[plan.first_block[seg] + start // plan.block + k] = got[
                        i * RANK:(i + 1) * RANK, k * plan.block:(k + 1) * plan.block]

        looped = [piece for piece in plan.pieces if piece[0] in (3, 7)]
        for arg, places, segs, width in plan.pieces:
            if (arg, places, segs, width) in looped:
                continue
            step = chunk_of(width, plan.block)
            left = left_of(arg, places)
            for start in range(0, width, step):
                one_part(arg, left, segs, start, step, copies[arg, start])
        lefts = [left_of(arg, places) for arg, places, _, _ in looped]
        step = chunk_of(looped[0][3], plan.block)

        def trip(n, carry):
            start = pl.multiple_of(n * step, LANES)
            for (arg, _, segs, _), left in zip(looped, lefts):
                view = (slice(None),) * (len(data[arg].shape) - 1) + (pl.ds(start, step),)
                copy = pltpu.make_async_copy(
                    data[arg].at[view], bufs[arg].at[view], sems.at[numbers[arg, 0] + n])
                one_part(arg, left, segs, start, step, copy)
            return carry

        lax.fori_loop(0, looped[0][3] // step, trip, 0)
        bit = (lax.axis_index("proj") >> split) & 1
        sent = pltpu.make_async_copy(grads.at[pl.ds((1 - bit) * half, half)], send, out_sems.at[0])
        kept = pltpu.make_async_copy(grads.at[pl.ds(bit * half, half)], keep, out_sems.at[1])
        sent.start()
        kept.start()
        finish()
        sent.wait()
        kept.wait()

    return kernel


def gradients(plan, data, own, other, mask, split, bases, first, count, so_far):
    anywhere = pl.BlockSpec(memory_space=pl.ANY)
    smem = pl.BlockSpec(memory_space=pltpu.SMEM)
    whole = pl.BlockSpec(memory_space=pltpu.VMEM)
    half = jax.ShapeDtypeStruct((plan.blocks // 2, RANK, plan.block), jnp.float32)
    return pl.pallas_call(
        gradient_kernel(plan, split, first, count),
        in_specs=[anywhere] * 9 + [whole] * 3 + [smem, anywhere],
        out_specs=[anywhere] * 3,
        out_shape=[half, half, jax.ShapeDtypeStruct(so_far.shape, so_far.dtype)],
        scratch_shapes=data_buffers(plan, data)
        + [
            pltpu.VMEM((plan.blocks, RANK, plan.block), jnp.float32),
            pltpu.SemaphoreType.DMA((copy_count(plan),)),
            pltpu.SemaphoreType.DMA((2,)),
        ]
        + fill_scratch(plan, count),
        input_output_aliases={13: 2},
        name="gradients",
    )(*data, own, other, mask, bases, so_far)


def row_offsets(plan):
    return lax.broadcasted_iota(jnp.int32, (plan.sub, LANES), 0) * wrapped(RANK * ROW_MULT)


def step_keys(step, bases, offsets):
    turn = wrapped(step % RANK * ROW_MULT) if isinstance(step, int) else (step % RANK) * ROW_MULT
    key = bases[step // RANK] + turn + offsets
    key = key ^ srl(key, 16)
    return jnp.concatenate([key] * (COLS // LANES), axis=1)


def column_keys(copies=1):
    cols = lax.broadcasted_iota(jnp.int32, (copies, K), 1) * COL_MULT
    return cols ^ srl(cols, 16)


def mixed(rows, cols):
    shape = rows.shape[0], cols.shape[1]
    h = rows.reshape(shape[0] // RANK, RANK, rows.shape[1]) ^ cols[None]
    h = h.reshape(shape) * MIX_A
    h = h ^ srl(h, 13)
    return h * MIX_B


def centred_sum(h):
    h = h ^ srl(h, 16)
    s = (h & 0x00FF00FF) + (srl(h, 8) | -0xFF0100)
    return (s * 0x10001).astype(jnp.float32).astype(jnp.bfloat16)


def byte_planes(h):
    low = h.astype(jnp.int16)
    high = srl(h, 16).astype(jnp.int16)
    low = low ^ high
    eight = jnp.int16(8)
    planes = [low, high, srl(low, eight), srl(high, eight)]
    return [p.astype(jnp.uint8).astype(jnp.bfloat16) for p in planes]


COLS = 256
LANES = 128
PAIR = 2
PART = 4608


def fill_step(step, bases, row_base, col_base, tile):
    rows = step_keys(step, bases, row_base[...])
    for c in range(0, K, COLS):
        part = centred_sum(mixed(rows, col_base[:, c:c + COLS]))
        for n in range(0, COLS, LANES):
            tile[(c + n) // LANES] = part[:, n:n + LANES]


def fill_tables(plan, first, count, refs, out):
    bases, row_base, col_base, tiles, sems = refs[:5]
    row_base[...] = row_offsets(plan)
    col_base[...] = column_keys(RANK)

    def body(n, carry):
        fill_step(n + first, bases, row_base, col_base, tiles.at[n])
        pltpu.make_async_copy(tiles.at[n], out.at[n + first], sems.at[n]).start()
        return carry

    lax.fori_loop(0, count, body, 0)

    def wait():
        for n in range(count):
            pltpu.make_async_copy(tiles.at[n], out.at[n + first], sems.at[n]).wait()

    return wait


def fill_scratch(plan, count):
    return [
        pltpu.VMEM((plan.sub, LANES), jnp.int32),
        pltpu.VMEM((RANK, K), jnp.int32),
        pltpu.VMEM((count, K // LANES, plan.sub, LANES), jnp.bfloat16),
        pltpu.SemaphoreType.DMA((count,)),
    ]


def tiles_shape(plan, total):
    return jax.ShapeDtypeStruct((total, K // LANES, plan.sub, LANES), jnp.bfloat16)


def stored_table(plan, bases, first, count, after, so_far):
    smem = pl.BlockSpec(memory_space=pltpu.SMEM)
    anywhere = pl.BlockSpec(memory_space=pl.ANY)

    def kernel(bases, after, so_far, out, *scratch):
        fill_tables(plan, first, count, (bases,) + scratch, out)()

    return pl.pallas_call(
        kernel,
        in_specs=[smem, anywhere, anywhere],
        out_specs=anywhere,
        out_shape=jax.ShapeDtypeStruct(so_far.shape, so_far.dtype),
        scratch_shapes=fill_scratch(plan, count),
        input_output_aliases={2: 0},
        name="stored_table",
    )(bases, after, so_far)


def project_kernel(plan, stored, scale, devices):
    rounds = (plan.steps - stored) // PAIR
    depth = 2 * RANK * plan.examples
    parts = 4
    slab = plan.sub // parts

    def pick(grads, step):
        rank = step % RANK
        rows = lax.broadcasted_iota(jnp.int32, (RANK, plan.sub), 0) == rank
        parts = []
        for e in range(plan.examples):
            g = jnp.where(rows, grads[e, 0], 0.0)
            top = g.astype(jnp.bfloat16).astype(jnp.float32)
            parts += [top, g - top]
        return rows_of(parts).astype(jnp.bfloat16)

    def kernel(bases, grads, old_grads, tiles, out, acc, row_base, col_base):
        i = pl.program_id(0)

        @pl.when(i == 0)
        def _():
            acc[...] = jnp.zeros_like(acc)
            row_base[...] = row_offsets(plan)
            col_base[...] = column_keys(RANK)

        old = pick(old_grads, i)
        old = jnp.where(i < stored, old.astype(jnp.float32), 0.0)
        fix = jnp.sum(old, axis=1, keepdims=True)
        old = (old * (1.0 / 65536.0)).astype(jnp.bfloat16)
        lefts, rows = [], []
        for p in range(PAIR):
            step = stored + PAIR * i + p
            rows.append(step_keys(step, bases, row_base[...]))
            left = pick(grads, step)
            fix = fix - 510.0 * jnp.sum(left.astype(jnp.float32), axis=1, keepdims=True)
            lefts.append([jnp.concatenate([left[:, b:b + slab]] * parts, axis=1) for b in range(0, plan.sub, slab)])
        for c in range(0, K, COLS):
            a = acc[:, c:c + COLS] + fix
            for p in range(PAIR):
                for n in range(parts):
                    planes = byte_planes(mixed(rows[p][n * slab:(n + 1) * slab], col_base[:, c:c + COLS]))
                    a = a + jnp.dot(lefts[p][n], rows_of(planes), preferred_element_type=jnp.float32)
            tile = jnp.concatenate([tiles[0, (c + n) // LANES] for n in range(0, COLS, LANES)], axis=1)
            a = a + jnp.dot(old, tile, preferred_element_type=jnp.float32)
            acc[:, c:c + COLS] = a

        @pl.when(i == rounds - 1)
        def _():
            width = K // devices
            for e in range(plan.examples):
                part = acc[e * 2 * RANK:(e + 1) * 2 * RANK, :]
                total = jnp.sum(part, axis=0, keepdims=True) * scale
                for d in range(devices):
                    out[d, e:e + 1, :] = total[:, d * width:(d + 1) * width]

    return kernel, depth, rounds


def project(plan, bases, grads, tiles, stored, scale, devices):
    kernel, depth, rounds = project_kernel(plan, stored, scale, devices)
    smem = pl.BlockSpec(memory_space=pltpu.SMEM)
    parts = plan.block // plan.sub

    def place(step):
        number = step // RANK
        return (0, number // parts, 0, number % parts)

    last = stored - 1
    return pl.pallas_call(
        kernel,
        grid=(rounds,),
        in_specs=[
            smem,
            pl.BlockSpec((plan.examples, 1, RANK, plan.sub), lambda i: place(PAIR * i + stored)),
            pl.BlockSpec((plan.examples, 1, RANK, plan.sub), lambda i: place(jnp.minimum(i, last))),
            pl.BlockSpec((1, K // LANES, plan.sub, LANES), lambda i: (jnp.minimum(i, last), 0, 0, 0)),
        ],
        out_specs=pl.BlockSpec((devices, plan.examples, K // devices), lambda i: (0, 0, 0)),
        out_shape=jax.ShapeDtypeStruct((devices, plan.examples, K // devices), jnp.float32),
        scratch_shapes=[
            pltpu.VMEM((depth, K), jnp.float32),
            pltpu.VMEM((plan.sub, LANES), jnp.int32),
            pltpu.VMEM((RANK, K), jnp.int32),
        ],
        name="project",
    )(bases, grads, grads, tiles)


def swap(x, axis, bit):
    size = lax.axis_size(axis)
    return lax.ppermute(x, axis, [(i, i ^ (1 << bit)) for i in range(size)])


def shards(*args):
    data = args[:9]
    factors = args[9:14]
    mask, seeds = args[14:16]
    plan = Plan(tuple(x.shape[-1] for x in data), data[0].shape[0], lax.axis_size("proj"))
    table = jnp.asarray(plan.table)
    counts = [max(1, c * plan.steps // 128) for c in STORED_STEPS][:6]
    counts[-1] += sum(counts) % PAIR
    starts = [sum(counts[:n]) for n in range(len(counts))]
    stored = sum(counts)
    own, tiles, bases = products(plan, data, factors, table, seeds, counts[0], stored)

    def cover(received, sent, number):
        nonlocal tiles
        tiles = stored_table(plan, bases, starts[number], counts[number], sent, tiles)
        received, tiles = lax.optimization_barrier((received, tiles))
        return received

    if lax.axis_size("mp") == 2:
        other = swap(own, "mp", 0)
    else:
        own = lax.psum(own, "mp")
        other = jnp.zeros_like(own)
    other = cover(other, own, 1)
    other = pltpu.with_memory_space_constraint(other, pltpu.VMEM)
    keep, send, tiles = gradients(
        plan, data, own, other, mask.reshape(1, -1), plan.bits[0], bases, starts[2], counts[2], tiles)
    j = lax.axis_index("proj")
    low = len(plan.bits[:2])
    x = None
    for number, bit in enumerate(plan.bits[:2]):
        if number > 0:
            half = x.shape[0] // 2
            side = (j >> bit) & 1
            send = lax.dynamic_slice_in_dim(x, (1 - side) * half, half, 0)
            keep = lax.dynamic_slice_in_dim(x, side * half, half, 0)
        received = cover(swap(send, "proj", bit), send, number + 3)
        x = keep + received
    ways = plan.group >> low
    if ways > 1:
        size = x.shape[0] // ways
        place = (j >> low) % ways
        sends = [lax.dynamic_slice_in_dim(x, (place ^ d) * size, size, 0) for d in range(ways)]
        got = [lax.ppermute(sends[d], "proj", [(i, i ^ (d << low)) for i in range(plan.owners)]) for d in range(1, ways)]
        got = cover(got, sends[0], low + 3)
        x = sends[0]
        for one in got:
            x = x + one
    x = x[None]
    if plan.examples > 1:
        groups = [[e * plan.group + i for e in range(plan.examples)] for i in range(plan.group)]
        x = x.reshape((plan.examples, plan.own_blocks) + x.shape[2:])
        x = lax.all_to_all(x, "proj", 0, 0, axis_index_groups=groups, tiled=True)
    scale = 1.0 / (LENGTH * math.sqrt(21845.0 * K))
    devices = lax.axis_size("mp") * plan.owners
    pieces = project(plan, bases, x, tiles, stored, scale, devices)
    got = lax.all_to_all(pieces, ("mp", "proj"), 0, 0, tiled=True)
    return got.sum(axis=0)


def solution(mesh):
    in_specs = (
        P("proj", "mp"),
        P("proj", "mp"),
        P("proj", "mp"),
        P("proj", "mp"),
        P("proj", "mp"),
        P("proj", None, "mp"),
        P("proj", "mp"),
        P("proj", None, "mp"),
        P("proj", "mp"),
        P(None, None, "mp"),
        P(None, "mp"),
        P(None, None, "mp"),
        P(None, None, "mp"),
        P(None, None, "mp"),
        P("proj"),
        P(),
    )
    out_specs = P(None, ("mp", "proj"))
    return jax.shard_map(shards, mesh=mesh, in_specs=in_specs, out_specs=out_specs, check_vma=False)
```

```python
import math

import jax
import jax.numpy as jnp
import numpy as np
from jax import lax
from jax.experimental import pallas as pl
from jax.experimental.pallas import tpu as pltpu
from jax.sharding import PartitionSpec as P

K = 2048
LENGTH = 2048
RANK = 8
ROWS = 256
SEED_MULT = 1103515245
ROW_MULT = 668265263
COL_MULT = -1640531535
MIX_A = -2048144789
MIX_B = -1028477387
STORED_STEPS = (5, 2, 5, 5, 11, 12)

srl = lax.shift_right_logical


def chunk_of(width, unit, limit=4608):
    for parts in range(1, width // unit + 1):
        if width % (parts * unit) == 0 and width // parts <= limit:
            return width // parts
    return width


def wrapped(number):
    return (number + 2**31) % 2**32 - 2**31


def rows_of(parts):
    return jnp.concatenate(parts, axis=0) if len(parts) > 1 else parts[0]


class Plan:
    def __init__(self, widths, tokens, owners):
        self.widths = widths
        self.tokens = tokens
        self.owners = owners
        hid, att, gin, dwn, qry, kvw, aow, guw, dow = widths
        self.pieces = [
            (0, (24, 32, 40), (0, 2, 4), hid),
            (4, (0,), (1,), qry),
            (5, (8, 16), (3, 5), kvw),
            (1, (56,), (6,), att),
            (6, (48,), (7,), aow),
            (2, (80, 88), (8, 10), gin),
            (7, (64, 72), (9, 11), guw),
            (3, (104,), (12,), dwn),
            (8, (96,), (13,), dow),
        ]
        self.block = 0
        for _, _, _, width in self.pieces:
            self.block = math.gcd(self.block, width)
        while self.block > 512:
            self.block //= 2
        seg_tab, off_tab, width_tab = [], [], []
        self.first_block = {}
        for _, _, segs, width in self.pieces:
            for seg in segs:
                self.first_block[seg] = len(seg_tab)
                for number in range(width // self.block):
                    seg_tab.append(seg)
                    off_tab.append(number * self.block)
                    width_tab.append(width)
        self.blocks = len(seg_tab)
        self.table = np.array([seg_tab, off_tab, width_tab], np.int32)
        self.group = LENGTH // tokens
        self.examples = owners // self.group
        self.own_blocks = self.blocks // owners
        self.sub = min(ROWS, self.block)
        self.steps = self.own_blocks * (self.block // self.sub) * RANK
        bits = self.group.bit_length() - 1
        self.bits = ([0, 1] + list(reversed(range(2, bits))))[:bits]

    def first_own(self):
        j = lax.axis_index("proj")
        piece = 0
        for bit in self.bits:
            piece = piece * 2 + ((j >> bit) & 1)
        return piece * (self.blocks // self.group) + (j // self.group) * self.own_blocks


def every_other(x, first):
    wide = x.shape[1]
    u = lax.broadcasted_iota(jnp.int32, (wide, wide // 2), 0)
    t = lax.broadcasted_iota(jnp.int32, (wide, wide // 2), 1)
    choose = (u == 2 * t + first).astype(jnp.float32).astype(jnp.bfloat16)
    total = None
    for _ in range(3):
        term = x.astype(jnp.bfloat16)
        x = x - term.astype(jnp.float32)
        got = jnp.dot(term, choose, preferred_element_type=jnp.float32)
        total = got if total is None else total + got
    return total


NARROW = (0, 4, 1, 6, 2, 8)
NARROW_ROWS = ((0, 24), (24, 8), (48, 8), (56, 8), (64, 16), (104, 8))


def product_kernel(plan, count):
    wide = plan.widths[3]
    part = chunk_of(wide, plan.block, PART)
    trips = wide // part

    def kernel(*refs):
        data = refs[:9]
        aif, daf, aof, kvb, gub = refs[9:14]
        table, seeds = refs[14:16]
        out, tiles, bases = refs[16:19]
        narrow, kv, gate_up, down, narrow_sems, wide_sems = refs[19:25]
        narrow_fac, kv_fac, gate_up_fac, down_fac, fac_sems = refs[25:30]
        fill_refs = (bases,) + refs[30:]
        pairs = [(aif.at[0], narrow_fac.at[0, pl.ds(0, RANK)]), (aif.at[1], narrow_fac.at[0, pl.ds(RANK, RANK)]),
                 (aif.at[2], narrow_fac.at[0, pl.ds(2 * RANK, RANK)]), (aof.at[0], narrow_fac.at[1, pl.ds(0, RANK)]),
                 (aif.at[3], narrow_fac.at[2, pl.ds(0, RANK)]), (aof.at[1], narrow_fac.at[3, pl.ds(0, RANK)]),
                 (aif.at[4], narrow_fac.at[4, pl.ds(0, RANK)]), (aif.at[5], narrow_fac.at[4, pl.ds(RANK, RANK)]),
                 (aof.at[2], narrow_fac.at[5, pl.ds(0, RANK)]), (daf, down_fac)]
        pairs += [(kvb.at[i], kv_fac.at[pl.ds(i * RANK, RANK)]) for i in range(2)]
        pairs += [(gub.at[i], gate_up_fac.at[pl.ds(i * RANK, RANK)]) for i in range(2)]
        loads = [pltpu.make_async_copy(x, y, fac_sems.at[n]) for n, (x, y) in enumerate(pairs)]
        loads += [pltpu.make_async_copy(data[arg], narrow.at[n], narrow_sems.at[n]) for n, arg in enumerate(NARROW)]
        loads.append(pltpu.make_async_copy(data[5], kv, narrow_sems.at[len(NARROW)]))

        def wide_copies(j):
            cols = pl.ds(pl.multiple_of(j * part, LANES), part)
            return [
                pltpu.make_async_copy(data[7].at[:, :, cols], gate_up.at[:, :, cols], wide_sems.at[0, j]),
                pltpu.make_async_copy(data[3].at[:, cols], down.at[:, cols], wide_sems.at[1, j]),
            ]

        for load in loads:
            load.start()

        def begin(j, carry):
            for copy in wide_copies(j):
                copy.start()
            return carry

        lax.fori_loop(0, trips, begin, 0)
        block = plan.first_own()
        for n in range(plan.steps // RANK):
            parts = plan.block // plan.sub
            seg = table[0, block + n // parts]
            feature = lax.axis_index("mp") * table[2, block + n // parts] + table[1, block + n // parts]
            feature = feature + (n % parts) * plan.sub
            bases[n] = seeds[seg] * SEED_MULT + feature * wrapped(RANK * ROW_MULT)

        def contract(left, right):
            return lax.dot_general(left, right, (((1,), (1,)), ((), ())), preferred_element_type=jnp.float32)

        def wide_part(j, carry):
            for copy in wide_copies(j):
                copy.wait()
            cols = pl.ds(pl.multiple_of(j * part, LANES), part)
            both = gate_up[:, :, cols].reshape(2 * plan.tokens, part)
            return carry[0] + contract(gate_up_fac[:, cols], both), carry[1] + contract(down_fac[:, cols], down[:, cols])

        zero = jnp.zeros((2 * RANK, 2 * plan.tokens), jnp.float32), jnp.zeros((RANK, plan.tokens), jnp.float32)
        finish = fill_tables(plan, 0, count, fill_refs, tiles)
        for load in loads:
            load.wait()

        def narrow_part(n, carry):
            sums[n] = contract(narrow_fac[n], narrow[n])
            return carry

        sums = refs[-1]
        lax.fori_loop(0, len(NARROW), narrow_part, 0)
        for n, (place, rows) in enumerate(NARROW_ROWS):
            out[place:place + rows, :] = sums[n, 0:rows]
        kv_sum = contract(kv_fac[...], kv[...].reshape(2 * plan.tokens, plan.widths[5]))
        gate_up_sum, down_sum = lax.fori_loop(0, trips, wide_part, zero)
        out[96:104, :] = down_sum
        for i in range(2):
            out[32 + i * RANK:32 + (i + 1) * RANK, :] = every_other(kv_sum[i * RANK:(i + 1) * RANK], i)
            out[80 + i * RANK:80 + (i + 1) * RANK, :] = every_other(gate_up_sum[i * RANK:(i + 1) * RANK], i)
        finish()

    return kernel


def copy_count(plan):
    return sum(width // chunk_of(width, plan.block) for width in plan.widths)


def data_buffers(plan, data):
    return [pltpu.VMEM(x.shape, jnp.bfloat16) for x in data]


def products(plan, data, factors, table, seeds, count, total):
    anywhere = pl.BlockSpec(memory_space=pl.ANY)
    smem = pl.BlockSpec(memory_space=pltpu.SMEM)
    whole = pl.BlockSpec(memory_space=pltpu.VMEM)
    return pl.pallas_call(
        product_kernel(plan, count),
        in_specs=[anywhere] * 14 + [smem, smem],
        out_specs=[whole, anywhere, smem],
        out_shape=[
            jax.ShapeDtypeStruct((14 * RANK, plan.tokens), jnp.float32),
            tiles_shape(plan, total),
            jax.ShapeDtypeStruct((plan.steps // RANK,), jnp.int32),
        ],
        scratch_shapes=[
            pltpu.VMEM((len(NARROW),) + data[0].shape, jnp.bfloat16),
            pltpu.VMEM(data[5].shape, jnp.bfloat16),
            pltpu.VMEM(data[7].shape, jnp.bfloat16),
            pltpu.VMEM(data[3].shape, jnp.bfloat16),
            pltpu.SemaphoreType.DMA((len(NARROW) + 1,)),
            pltpu.SemaphoreType.DMA((2, plan.widths[3] // chunk_of(plan.widths[3], plan.block, PART))),
            pltpu.VMEM((len(NARROW), 3 * RANK, plan.widths[0]), jnp.bfloat16),
            pltpu.VMEM((2 * RANK, plan.widths[5]), jnp.bfloat16),
            pltpu.VMEM((2 * RANK, plan.widths[7]), jnp.bfloat16),
            pltpu.VMEM((RANK, plan.widths[3]), jnp.bfloat16),
            pltpu.SemaphoreType.DMA((14,)),
        ]
        + fill_scratch(plan, count)
        + [pltpu.VMEM((len(NARROW), 3 * RANK, plan.tokens), jnp.float32)],
        name="products",
    )(*data, *factors, table, seeds)


def gradient_kernel(plan, split, first, count):
    def kernel(*refs):
        data = refs[:9]
        own, other, mask = refs[9:12]
        bases = refs[12]
        keep, send, tiles = refs[14:17]
        bufs = refs[17:26]
        grads, sems, out_sems = refs[26:29]
        fill_refs = (bases,) + refs[29:]
        copies = {}
        number = 0
        for arg, _, _, width in plan.pieces:
            step = chunk_of(width, plan.block)
            for start in range(0, width, step):
                view = (slice(None),) * (len(data[arg].shape) - 1) + (pl.ds(start, step),)
                copies[arg, start] = pltpu.make_async_copy(data[arg].at[view], bufs[arg].at[view], sems.at[number])
                number += 1
        for copy in copies.values():
            copy.start()
        finish = fill_tables(plan, first, count, fill_refs, tiles)
        total = own[...] + other[...]
        turned = total * mask[...].astype(jnp.float32)
        tokens = plan.tokens
        half = plan.blocks // 2
        for arg, places, segs, width in plan.pieces:
            left = rows_of([turned[p:p + RANK] for p in places]).astype(jnp.bfloat16)
            if len(data[arg].shape) == 3:
                t = lax.broadcasted_iota(jnp.int32, (tokens, 2 * tokens), 0)
                u = lax.broadcasted_iota(jnp.int32, (tokens, 2 * tokens), 1)
                parts = []
                for i in range(2):
                    spread = (u == 2 * t + i).astype(jnp.float32).astype(jnp.bfloat16)
                    one = turned[places[i]:places[i] + RANK].astype(jnp.bfloat16)
                    parts.append(jnp.dot(one, spread, preferred_element_type=jnp.float32))
                left = rows_of(parts).astype(jnp.bfloat16)
            step = chunk_of(width, plan.block)
            for start in range(0, width, step):
                copies[arg, start].wait()
                cols = pl.ds(start, step)
                if len(data[arg].shape) == 3:
                    right = bufs[arg][:, :, cols].reshape(2 * tokens, step)
                else:
                    right = bufs[arg][:, cols]
                got = jnp.dot(left, right, preferred_element_type=jnp.float32)
                for i, seg in enumerate(segs):
                    for k in range(step // plan.block):
                        block = plan.first_block[seg] + start // plan.block + k
                        grads[block // half, block % half] = got[
                            i * RANK:(i + 1) * RANK, k * plan.block:(k + 1) * plan.block]
        bit = (lax.axis_index("proj") >> split) & 1
        sent = pltpu.make_async_copy(grads.at[1 - bit], send, out_sems.at[0])
        kept = pltpu.make_async_copy(grads.at[bit], keep, out_sems.at[1])
        sent.start()
        kept.start()
        finish()
        sent.wait()
        kept.wait()

    return kernel


def gradients(plan, data, own, other, mask, split, bases, first, count, so_far):
    anywhere = pl.BlockSpec(memory_space=pl.ANY)
    smem = pl.BlockSpec(memory_space=pltpu.SMEM)
    whole = pl.BlockSpec(memory_space=pltpu.VMEM)
    half = jax.ShapeDtypeStruct((plan.blocks // 2, RANK, plan.block), jnp.float32)
    return pl.pallas_call(
        gradient_kernel(plan, split, first, count),
        in_specs=[anywhere] * 9 + [whole] * 3 + [smem, anywhere],
        out_specs=[anywhere] * 3,
        out_shape=[half, half, jax.ShapeDtypeStruct(so_far.shape, so_far.dtype)],
        scratch_shapes=data_buffers(plan, data)
        + [
            pltpu.VMEM((2, plan.blocks // 2, RANK, plan.block), jnp.float32),
            pltpu.SemaphoreType.DMA((copy_count(plan),)),
            pltpu.SemaphoreType.DMA((2,)),
        ]
        + fill_scratch(plan, count),
        input_output_aliases={13: 2},
        name="gradients",
    )(*data, own, other, mask, bases, so_far)


def row_offsets(plan):
    return lax.broadcasted_iota(jnp.int32, (plan.sub, LANES), 0) * wrapped(RANK * ROW_MULT)


def step_keys(step, bases, offsets):
    turn = wrapped(step % RANK * ROW_MULT) if isinstance(step, int) else (step % RANK) * ROW_MULT
    key = bases[step // RANK] + turn + offsets
    key = key ^ srl(key, 16)
    return jnp.concatenate([key] * (COLS // LANES), axis=1)


def column_keys(copies=1):
    cols = lax.broadcasted_iota(jnp.int32, (copies, K), 1) * COL_MULT
    return cols ^ srl(cols, 16)


def mixed(rows, cols):
    shape = rows.shape[0], cols.shape[1]
    h = rows.reshape(shape[0] // RANK, RANK, rows.shape[1]) ^ cols[None]
    h = h.reshape(shape) * MIX_A
    h = h ^ srl(h, 13)
    return h * MIX_B


def centred_sum(h):
    h = h ^ srl(h, 16)
    s = (h & 0x00FF00FF) + (srl(h, 8) | -0xFF0100)
    return (s * 0x10001).astype(jnp.float32).astype(jnp.bfloat16)


def byte_planes(h):
    low = h.astype(jnp.int16)
    high = srl(h, 16).astype(jnp.int16)
    low = low ^ high
    eight = jnp.int16(8)
    planes = [low, high, srl(low, eight), srl(high, eight)]
    return [p.astype(jnp.uint8).astype(jnp.bfloat16) for p in planes]


COLS = 256
LANES = 128
PAIR = 4
PART = 4608


def fill_step(step, bases, row_base, col_base, tile):
    rows = step_keys(step, bases, row_base[...])
    for c in range(0, K, COLS):
        part = centred_sum(mixed(rows, col_base[:, c:c + COLS]))
        for n in range(0, COLS, LANES):
            tile[(c + n) // LANES] = part[:, n:n + LANES]


def fill_tables(plan, first, count, refs, out):
    bases, row_base, col_base, tiles, sems = refs[:5]
    row_base[...] = row_offsets(plan)
    col_base[...] = column_keys(RANK)

    def body(n, carry):
        fill_step(n + first, bases, row_base, col_base, tiles.at[n])
        pltpu.make_async_copy(tiles.at[n], out.at[n + first], sems.at[n]).start()
        return carry

    lax.fori_loop(0, count, body, 0)

    def wait():
        for n in range(count):
            pltpu.make_async_copy(tiles.at[n], out.at[n + first], sems.at[n]).wait()

    return wait


def fill_scratch(plan, count):
    return [
        pltpu.VMEM((plan.sub, LANES), jnp.int32),
        pltpu.VMEM((RANK, K), jnp.int32),
        pltpu.VMEM((count, K // LANES, plan.sub, LANES), jnp.bfloat16),
        pltpu.SemaphoreType.DMA((count,)),
    ]


def tiles_shape(plan, total):
    return jax.ShapeDtypeStruct((total, K // LANES, plan.sub, LANES), jnp.bfloat16)


def stored_table(plan, bases, first, count, after, so_far):
    smem = pl.BlockSpec(memory_space=pltpu.SMEM)
    anywhere = pl.BlockSpec(memory_space=pl.ANY)

    def kernel(bases, after, so_far, out, *scratch):
        fill_tables(plan, first, count, (bases,) + scratch, out)()

    return pl.pallas_call(
        kernel,
        in_specs=[smem, anywhere, anywhere],
        out_specs=anywhere,
        out_shape=jax.ShapeDtypeStruct(so_far.shape, so_far.dtype),
        scratch_shapes=fill_scratch(plan, count),
        input_output_aliases={2: 0},
        name="stored_table",
    )(bases, after, so_far)


def round_sizes(plan, stored):
    rounds = (plan.steps - stored) // PAIR
    batch = 1
    while batch * rounds < stored:
        batch *= 2
    return rounds, batch


def project_kernel(plan, stored, scale, devices):
    rounds, batch = round_sizes(plan, stored)
    depth = 2 * RANK * plan.examples
    parts = 4
    slab = plan.sub // parts

    def pick(grads, step):
        rank = step % RANK
        rows = lax.broadcasted_iota(jnp.int32, (RANK, plan.sub), 0) == rank
        parts = []
        for e in range(plan.examples):
            g = jnp.where(rows, grads[e, 0], 0.0)
            top = g.astype(jnp.bfloat16).astype(jnp.float32)
            parts += [top, g - top]
        return rows_of(parts).astype(jnp.bfloat16)

    def kernel(bases, grads, old_grads, tiles, out, acc, row_base, col_base):
        i = pl.program_id(0)

        @pl.when(i == 0)
        def _():
            acc[...] = jnp.zeros_like(acc)
            row_base[...] = row_offsets(plan)
            col_base[...] = column_keys(RANK)

        fix = 0.0
        olds, lefts, rows = [], [], []
        for q in range(batch):
            old = pick(old_grads, batch * i + q)
            old = jnp.where(batch * i + q < stored, old.astype(jnp.float32), 0.0)
            fix = fix + jnp.sum(old, axis=1, keepdims=True)
            olds.append((old * (1.0 / 65536.0)).astype(jnp.bfloat16))
        for p in range(PAIR):
            step = stored + PAIR * i + p
            rows.append(step_keys(step, bases, row_base[...]))
            left = pick(grads, step)
            fix = fix - 510.0 * jnp.sum(left.astype(jnp.float32), axis=1, keepdims=True)
            lefts.append([jnp.concatenate([left[:, b:b + slab]] * parts, axis=1) for b in range(0, plan.sub, slab)])
        for c in range(0, K, COLS):
            a = acc[:, c:c + COLS] + fix
            for p in range(PAIR):
                for n in range(parts):
                    planes = byte_planes(mixed(rows[p][n * slab:(n + 1) * slab], col_base[:, c:c + COLS]))
                    a = a + jnp.dot(lefts[p][n], rows_of(planes), preferred_element_type=jnp.float32)
            for q in range(batch):
                tile = jnp.concatenate([tiles[q, (c + n) // LANES] for n in range(0, COLS, LANES)], axis=1)
                a = a + jnp.dot(olds[q], tile, preferred_element_type=jnp.float32)
            acc[:, c:c + COLS] = a

        @pl.when(i == rounds - 1)
        def _():
            width = K // devices
            for e in range(plan.examples):
                part = acc[e * 2 * RANK:(e + 1) * 2 * RANK, :]
                total = jnp.sum(part, axis=0, keepdims=True) * scale
                for d in range(devices):
                    out[d, e:e + 1, :] = total[:, d * width:(d + 1) * width]

    return kernel, depth, rounds, batch


def project(plan, bases, grads, tiles, stored, scale, devices):
    kernel, depth, rounds, batch = project_kernel(plan, stored, scale, devices)
    smem = pl.BlockSpec(memory_space=pltpu.SMEM)
    parts = plan.block // plan.sub

    def place(step):
        number = step // RANK
        return (0, number // parts, 0, number % parts)

    last = stored // batch - 1
    return pl.pallas_call(
        kernel,
        grid=(rounds,),
        in_specs=[
            smem,
            pl.BlockSpec((plan.examples, 1, RANK, plan.sub), lambda i: place(PAIR * i + stored)),
            pl.BlockSpec((plan.examples, 1, RANK, plan.sub), lambda i: place(jnp.minimum(i, last) * batch)),
            pl.BlockSpec((batch, K // LANES, plan.sub, LANES), lambda i: (jnp.minimum(i, last), 0, 0, 0)),
        ],
        out_specs=pl.BlockSpec((devices, plan.examples, K // devices), lambda i: (0, 0, 0)),
        out_shape=jax.ShapeDtypeStruct((devices, plan.examples, K // devices), jnp.float32),
        scratch_shapes=[
            pltpu.VMEM((depth, K), jnp.float32),
            pltpu.VMEM((plan.sub, LANES), jnp.int32),
            pltpu.VMEM((RANK, K), jnp.int32),
        ],
        name="project",
    )(bases, grads, grads, tiles)


def swap(x, axis, bit):
    size = lax.axis_size(axis)
    return lax.ppermute(x, axis, [(i, i ^ (1 << bit)) for i in range(size)])


def shards(*args):
    data = args[:9]
    factors = args[9:14]
    mask, seeds = args[14:16]
    plan = Plan(tuple(x.shape[-1] for x in data), data[0].shape[0], lax.axis_size("proj"))
    table = jnp.asarray(plan.table)
    counts = [max(1, c * plan.steps // 128) for c in STORED_STEPS][:6]
    counts[-1] += -sum(counts) % PAIR
    starts = [sum(counts[:n]) for n in range(len(counts))]
    stored = sum(counts)
    own, tiles, bases = products(plan, data, factors, table, seeds, counts[0], stored)

    def cover(received, sent, number):
        nonlocal tiles
        tiles = stored_table(plan, bases, starts[number], counts[number], sent, tiles)
        received, tiles = lax.optimization_barrier((received, tiles))
        return received

    if lax.axis_size("mp") == 2:
        other = swap(own, "mp", 0)
    else:
        own = lax.psum(own, "mp")
        other = jnp.zeros_like(own)
    other = cover(other, own, 1)
    other = pltpu.with_memory_space_constraint(other, pltpu.VMEM)
    keep, send, tiles = gradients(
        plan, data, own, other, mask.reshape(1, -1), plan.bits[0], bases, starts[2], counts[2], tiles)
    j = lax.axis_index("proj")
    low = len(plan.bits[:2])
    x = None
    for number, bit in enumerate(plan.bits[:2]):
        if number > 0:
            half = x.shape[0] // 2
            side = (j >> bit) & 1
            send = lax.dynamic_slice_in_dim(x, (1 - side) * half, half, 0)
            keep = lax.dynamic_slice_in_dim(x, side * half, half, 0)
        received = cover(swap(send, "proj", bit), send, number + 3)
        x = keep + received
    ways = plan.group >> low
    if ways > 1:
        size = x.shape[0] // ways
        place = (j >> low) % ways
        sends = [lax.dynamic_slice_in_dim(x, (place ^ d) * size, size, 0) for d in range(ways)]
        got = [lax.ppermute(sends[d], "proj", [(i, i ^ (d << low)) for i in range(plan.owners)]) for d in range(1, ways)]
        got = cover(got, sends[0], low + 3)
        x = sends[0]
        for one in got:
            x = x + one
    x = x[None]
    if plan.examples > 1:
        groups = [[e * plan.group + i for e in range(plan.examples)] for i in range(plan.group)]
        x = x.reshape((plan.examples, plan.own_blocks) + x.shape[2:])
        x = lax.all_to_all(x, "proj", 0, 0, axis_index_groups=groups, tiled=True)
    scale = 1.0 / (LENGTH * math.sqrt(21845.0 * K))
    devices = lax.axis_size("mp") * plan.owners
    pieces = project(plan, bases, x, tiles, stored, scale, devices)
    got = lax.all_to_all(pieces, ("mp", "proj"), 0, 0, tiled=True)
    return got.sum(axis=0)


def solution(mesh):
    in_specs = (
        P("proj", "mp"),
        P("proj", "mp"),
        P("proj", "mp"),
        P("proj", "mp"),
        P("proj", "mp"),
        P("proj", None, "mp"),
        P("proj", "mp"),
        P("proj", None, "mp"),
        P("proj", "mp"),
        P(None, None, "mp"),
        P(None, "mp"),
        P(None, None, "mp"),
        P(None, None, "mp"),
        P(None, None, "mp"),
        P("proj"),
        P(),
    )
    out_specs = P(None, ("mp", "proj"))
    return jax.shard_map(shards, mesh=mesh, in_specs=in_specs, out_specs=out_specs, check_vma=False)
```

```python
import math

import jax
import jax.numpy as jnp
import numpy as np
from jax import lax
from jax.experimental import pallas as pl
from jax.experimental.pallas import tpu as pltpu
from jax.sharding import PartitionSpec as P

K = 2048
LENGTH = 2048
RANK = 8
ROWS = 256
SEED_MULT = 1103515245
ROW_MULT = 668265263
COL_MULT = -1640531535
MIX_A = -2048144789
MIX_B = -1028477387
STORED_STEPS = (5, 2, 5, 3, 10, 11)

srl = lax.shift_right_logical


def chunk_of(width, unit, limit=4608):
    for parts in range(1, width // unit + 1):
        if width % (parts * unit) == 0 and width // parts <= limit:
            return width // parts
    return width


def wrapped(number):
    return (number + 2**31) % 2**32 - 2**31


def rows_of(parts):
    return jnp.concatenate(parts, axis=0) if len(parts) > 1 else parts[0]


class Plan:
    def __init__(self, widths, tokens, owners):
        self.widths = widths
        self.tokens = tokens
        self.owners = owners
        hid, att, gin, dwn, qry, kvw, aow, guw, dow = widths
        self.pieces = [
            (0, (24, 32, 40), (0, 2, 4), hid),
            (4, (0,), (1,), qry),
            (5, (8, 16), (3, 5), kvw),
            (1, (56,), (6,), att),
            (6, (48,), (7,), aow),
            (2, (80, 88), (8, 10), gin),
            (7, (64, 72), (9, 11), guw),
            (3, (104,), (12,), dwn),
            (8, (96,), (13,), dow),
        ]
        self.block = 0
        for _, _, _, width in self.pieces:
            self.block = math.gcd(self.block, width)
        while self.block > 512:
            self.block //= 2
        seg_tab, off_tab, width_tab = [], [], []
        self.first_block = {}
        for _, _, segs, width in self.pieces:
            for seg in segs:
                self.first_block[seg] = len(seg_tab)
                for number in range(width // self.block):
                    seg_tab.append(seg)
                    off_tab.append(number * self.block)
                    width_tab.append(width)
        self.blocks = len(seg_tab)
        self.table = np.array([seg_tab, off_tab, width_tab], np.int32)
        self.group = LENGTH // tokens
        self.examples = owners // self.group
        self.own_blocks = self.blocks // owners
        self.sub = min(ROWS, self.block)
        self.steps = self.own_blocks * (self.block // self.sub) * RANK
        bits = self.group.bit_length() - 1
        self.bits = ([0, 1] + list(reversed(range(2, bits))))[:bits]

    def first_own(self):
        j = lax.axis_index("proj")
        piece = 0
        for bit in self.bits:
            piece = piece * 2 + ((j >> bit) & 1)
        return piece * (self.blocks // self.group) + (j // self.group) * self.own_blocks


def every_other(x, first):
    wide = x.shape[1]
    u = lax.broadcasted_iota(jnp.int32, (wide, wide // 2), 0)
    t = lax.broadcasted_iota(jnp.int32, (wide, wide // 2), 1)
    choose = (u == 2 * t + first).astype(jnp.float32).astype(jnp.bfloat16)
    total = None
    for _ in range(3):
        term = x.astype(jnp.bfloat16)
        x = x - term.astype(jnp.float32)
        got = jnp.dot(term, choose, preferred_element_type=jnp.float32)
        total = got if total is None else total + got
    return total


NARROW = (0, 4, 1, 6, 2, 8)
NARROW_ROWS = ((0, 24), (24, 8), (48, 8), (56, 8), (64, 16), (104, 8))


def product_kernel(plan, count):
    wide = plan.widths[3]
    part = chunk_of(wide, plan.block, PART)
    trips = wide // part

    def kernel(*refs):
        data = refs[:9]
        aif, daf, aof, kvb, gub = refs[9:14]
        table, seeds = refs[14:16]
        out, tiles, bases = refs[16:19]
        narrow, kv, gate_up, down, narrow_sems, wide_sems = refs[19:25]
        narrow_fac, kv_fac, gate_up_fac, down_fac, fac_sems = refs[25:30]
        fill_refs = (bases,) + refs[30:]
        pairs = [(aif.at[0], narrow_fac.at[0, pl.ds(0, RANK)]), (aif.at[1], narrow_fac.at[0, pl.ds(RANK, RANK)]),
                 (aif.at[2], narrow_fac.at[0, pl.ds(2 * RANK, RANK)]), (aof.at[0], narrow_fac.at[1, pl.ds(0, RANK)]),
                 (aif.at[3], narrow_fac.at[2, pl.ds(0, RANK)]), (aof.at[1], narrow_fac.at[3, pl.ds(0, RANK)]),
                 (aif.at[4], narrow_fac.at[4, pl.ds(0, RANK)]), (aif.at[5], narrow_fac.at[4, pl.ds(RANK, RANK)]),
                 (aof.at[2], narrow_fac.at[5, pl.ds(0, RANK)]), (daf, down_fac)]
        pairs += [(kvb.at[i], kv_fac.at[pl.ds(i * RANK, RANK)]) for i in range(2)]
        pairs += [(gub.at[i], gate_up_fac.at[pl.ds(i * RANK, RANK)]) for i in range(2)]
        loads = [pltpu.make_async_copy(x, y, fac_sems.at[n]) for n, (x, y) in enumerate(pairs)]
        loads += [pltpu.make_async_copy(data[arg], narrow.at[n], narrow_sems.at[n]) for n, arg in enumerate(NARROW)]
        loads.append(pltpu.make_async_copy(data[5], kv, narrow_sems.at[len(NARROW)]))

        def wide_copies(j):
            cols = pl.ds(pl.multiple_of(j * part, LANES), part)
            return [
                pltpu.make_async_copy(data[7].at[:, :, cols], gate_up.at[:, :, cols], wide_sems.at[0, j]),
                pltpu.make_async_copy(data[3].at[:, cols], down.at[:, cols], wide_sems.at[1, j]),
            ]

        for load in loads:
            load.start()

        def begin(j, carry):
            for copy in wide_copies(j):
                copy.start()
            return carry

        lax.fori_loop(0, trips, begin, 0)
        block = plan.first_own()
        for n in range(plan.steps // RANK):
            parts = plan.block // plan.sub
            seg = table[0, block + n // parts]
            feature = lax.axis_index("mp") * table[2, block + n // parts] + table[1, block + n // parts]
            feature = feature + (n % parts) * plan.sub
            bases[n] = seeds[seg] * SEED_MULT + feature * wrapped(RANK * ROW_MULT)

        def contract(left, right):
            return lax.dot_general(left, right, (((1,), (1,)), ((), ())), preferred_element_type=jnp.float32)

        def wide_part(j, carry):
            for copy in wide_copies(j):
                copy.wait()
            cols = pl.ds(pl.multiple_of(j * part, LANES), part)
            both = gate_up[:, :, cols].reshape(2 * plan.tokens, part)
            return carry[0] + contract(gate_up_fac[:, cols], both), carry[1] + contract(down_fac[:, cols], down[:, cols])

        zero = jnp.zeros((2 * RANK, 2 * plan.tokens), jnp.float32), jnp.zeros((RANK, plan.tokens), jnp.float32)
        finish = fill_tables(plan, 0, count, fill_refs, tiles)
        for load in loads:
            load.wait()

        def narrow_part(n, carry):
            sums[n] = contract(narrow_fac[n], narrow[n])
            return carry

        sums = refs[-1]
        lax.fori_loop(0, len(NARROW), narrow_part, 0)
        for n, (place, rows) in enumerate(NARROW_ROWS):
            out[place:place + rows, :] = sums[n, 0:rows]
        kv_sum = contract(kv_fac[...], kv[...].reshape(2 * plan.tokens, plan.widths[5]))
        gate_up_sum, down_sum = lax.fori_loop(0, trips, wide_part, zero)
        out[96:104, :] = down_sum
        for i in range(2):
            out[32 + i * RANK:32 + (i + 1) * RANK, :] = every_other(kv_sum[i * RANK:(i + 1) * RANK], i)
            out[80 + i * RANK:80 + (i + 1) * RANK, :] = every_other(gate_up_sum[i * RANK:(i + 1) * RANK], i)
        finish()

    return kernel


def copy_count(plan):
    return sum(width // chunk_of(width, plan.block) for width in plan.widths)


def data_buffers(plan, data):
    return [pltpu.VMEM(x.shape, jnp.bfloat16) for x in data]


def products(plan, data, factors, table, seeds, count, total):
    anywhere = pl.BlockSpec(memory_space=pl.ANY)
    smem = pl.BlockSpec(memory_space=pltpu.SMEM)
    whole = pl.BlockSpec(memory_space=pltpu.VMEM)
    return pl.pallas_call(
        product_kernel(plan, count),
        in_specs=[anywhere] * 14 + [smem, smem],
        out_specs=[whole, anywhere, smem],
        out_shape=[
            jax.ShapeDtypeStruct((14 * RANK, plan.tokens), jnp.float32),
            tiles_shape(plan, total),
            jax.ShapeDtypeStruct((plan.steps // RANK,), jnp.int32),
        ],
        scratch_shapes=[
            pltpu.VMEM((len(NARROW),) + data[0].shape, jnp.bfloat16),
            pltpu.VMEM(data[5].shape, jnp.bfloat16),
            pltpu.VMEM(data[7].shape, jnp.bfloat16),
            pltpu.VMEM(data[3].shape, jnp.bfloat16),
            pltpu.SemaphoreType.DMA((len(NARROW) + 1,)),
            pltpu.SemaphoreType.DMA((2, plan.widths[3] // chunk_of(plan.widths[3], plan.block, PART))),
            pltpu.VMEM((len(NARROW), 3 * RANK, plan.widths[0]), jnp.bfloat16),
            pltpu.VMEM((2 * RANK, plan.widths[5]), jnp.bfloat16),
            pltpu.VMEM((2 * RANK, plan.widths[7]), jnp.bfloat16),
            pltpu.VMEM((RANK, plan.widths[3]), jnp.bfloat16),
            pltpu.SemaphoreType.DMA((14,)),
        ]
        + fill_scratch(plan, count)
        + [pltpu.VMEM((len(NARROW), 3 * RANK, plan.tokens), jnp.float32)],
        name="products",
    )(*data, *factors, table, seeds)


def gradient_kernel(plan, split, first, count):
    def kernel(*refs):
        data = refs[:9]
        own, other, mask = refs[9:12]
        bases = refs[12]
        keep, send, tiles = refs[14:17]
        bufs = refs[17:26]
        grads, sems, out_sems = refs[26:29]
        fill_refs = (bases,) + refs[29:]
        copies = {}
        number = 0
        for arg, _, _, width in plan.pieces:
            step = chunk_of(width, plan.block)
            for start in range(0, width, step):
                view = (slice(None),) * (len(data[arg].shape) - 1) + (pl.ds(start, step),)
                copies[arg, start] = pltpu.make_async_copy(data[arg].at[view], bufs[arg].at[view], sems.at[number])
                number += 1
        for copy in copies.values():
            copy.start()
        finish = fill_tables(plan, first, count, fill_refs, tiles)
        total = own[...] + other[...]
        turned = total * mask[...].astype(jnp.float32)
        tokens = plan.tokens
        half = plan.blocks // 2
        for arg, places, segs, width in plan.pieces:
            left = rows_of([turned[p:p + RANK] for p in places]).astype(jnp.bfloat16)
            if len(data[arg].shape) == 3:
                t = lax.broadcasted_iota(jnp.int32, (tokens, 2 * tokens), 0)
                u = lax.broadcasted_iota(jnp.int32, (tokens, 2 * tokens), 1)
                parts = []
                for i in range(2):
                    spread = (u == 2 * t + i).astype(jnp.float32).astype(jnp.bfloat16)
                    one = turned[places[i]:places[i] + RANK].astype(jnp.bfloat16)
                    parts.append(jnp.dot(one, spread, preferred_element_type=jnp.float32))
                left = rows_of(parts).astype(jnp.bfloat16)
            step = chunk_of(width, plan.block)
            for start in range(0, width, step):
                copies[arg, start].wait()
                cols = pl.ds(start, step)
                if len(data[arg].shape) == 3:
                    right = bufs[arg][:, :, cols].reshape(2 * tokens, step)
                else:
                    right = bufs[arg][:, cols]
                got = jnp.dot(left, right, preferred_element_type=jnp.float32)
                for i, seg in enumerate(segs):
                    for k in range(step // plan.block):
                        block = plan.first_block[seg] + start // plan.block + k
                        grads[block // half, block % half] = got[
                            i * RANK:(i + 1) * RANK, k * plan.block:(k + 1) * plan.block]
        bit = (lax.axis_index("proj") >> split) & 1
        sent = pltpu.make_async_copy(grads.at[1 - bit], send, out_sems.at[0])
        kept = pltpu.make_async_copy(grads.at[bit], keep, out_sems.at[1])
        sent.start()
        kept.start()
        finish()
        sent.wait()
        kept.wait()

    return kernel


def gradients(plan, data, own, other, mask, split, bases, first, count, so_far):
    anywhere = pl.BlockSpec(memory_space=pl.ANY)
    smem = pl.BlockSpec(memory_space=pltpu.SMEM)
    whole = pl.BlockSpec(memory_space=pltpu.VMEM)
    half = jax.ShapeDtypeStruct((plan.blocks // 2, RANK, plan.block), jnp.float32)
    return pl.pallas_call(
        gradient_kernel(plan, split, first, count),
        in_specs=[anywhere] * 9 + [whole] * 3 + [smem, anywhere],
        out_specs=[anywhere] * 3,
        out_shape=[half, half, jax.ShapeDtypeStruct(so_far.shape, so_far.dtype)],
        scratch_shapes=data_buffers(plan, data)
        + [
            pltpu.VMEM((2, plan.blocks // 2, RANK, plan.block), jnp.float32),
            pltpu.SemaphoreType.DMA((copy_count(plan),)),
            pltpu.SemaphoreType.DMA((2,)),
        ]
        + fill_scratch(plan, count),
        input_output_aliases={13: 2},
        name="gradients",
    )(*data, own, other, mask, bases, so_far)


def row_offsets(plan):
    return lax.broadcasted_iota(jnp.int32, (plan.sub, LANES), 0) * wrapped(RANK * ROW_MULT)


def step_keys(step, bases, offsets):
    turn = wrapped(step % RANK * ROW_MULT) if isinstance(step, int) else (step % RANK) * ROW_MULT
    key = bases[step // RANK] + turn + offsets
    key = key ^ srl(key, 16)
    return jnp.concatenate([key] * (COLS // LANES), axis=1)


def column_keys(copies=1):
    cols = lax.broadcasted_iota(jnp.int32, (copies, K), 1) * COL_MULT
    return cols ^ srl(cols, 16)


def mixed(rows, cols):
    shape = rows.shape[0], cols.shape[1]
    h = rows.reshape(shape[0] // RANK, RANK, rows.shape[1]) ^ cols[None]
    h = h.reshape(shape) * MIX_A
    h = h ^ srl(h, 13)
    return h * MIX_B


def centred_sum(h):
    h = h ^ srl(h, 16)
    s = (h & 0x00FF00FF) + (srl(h, 8) | -0xFF0100)
    return (s * 0x10001).astype(jnp.float32).astype(jnp.bfloat16)


def byte_planes(h):
    low = h.astype(jnp.int16)
    high = srl(h, 16).astype(jnp.int16)
    low = low ^ high
    eight = jnp.int16(8)
    planes = [low, high, srl(low, eight), srl(high, eight)]
    return [p.astype(jnp.uint8).astype(jnp.bfloat16) for p in planes]


COLS = 256
LANES = 128
PAIR = 4
PART = 4608


def fill_step(step, bases, row_base, col_base, tile):
    rows = step_keys(step, bases, row_base[...])
    for c in range(0, K, COLS):
        part = centred_sum(mixed(rows, col_base[:, c:c + COLS]))
        for n in range(0, COLS, LANES):
            tile[(c + n) // LANES] = part[:, n:n + LANES]


def fill_tables(plan, first, count, refs, out):
    bases, row_base, col_base, tiles, sems = refs[:5]
    row_base[...] = row_offsets(plan)
    col_base[...] = column_keys(RANK)

    def body(n, carry):
        fill_step(n + first, bases, row_base, col_base, tiles.at[n])
        pltpu.make_async_copy(tiles.at[n], out.at[n + first], sems.at[n]).start()
        return carry

    lax.fori_loop(0, count, body, 0)

    def wait():
        for n in range(count):
            pltpu.make_async_copy(tiles.at[n], out.at[n + first], sems.at[n]).wait()

    return wait


def fill_scratch(plan, count):
    return [
        pltpu.VMEM((plan.sub, LANES), jnp.int32),
        pltpu.VMEM((RANK, K), jnp.int32),
        pltpu.VMEM((count, K // LANES, plan.sub, LANES), jnp.bfloat16),
        pltpu.SemaphoreType.DMA((count,)),
    ]


def tiles_shape(plan, total):
    return jax.ShapeDtypeStruct((total, K // LANES, plan.sub, LANES), jnp.bfloat16)


def stored_table(plan, bases, first, count, after, so_far, in_vmem):
    smem = pl.BlockSpec(memory_space=pltpu.SMEM)
    anywhere = pl.BlockSpec(memory_space=pl.ANY)
    place = anywhere
    if in_vmem:
        after = pltpu.with_memory_space_constraint(after, pltpu.VMEM)
        place = pl.BlockSpec(memory_space=pltpu.VMEM)

    def kernel(bases, after, so_far, out, *scratch):
        fill_tables(plan, first, count, (bases,) + scratch, out)()

    return pl.pallas_call(
        kernel,
        in_specs=[smem, place, anywhere],
        out_specs=anywhere,
        out_shape=jax.ShapeDtypeStruct(so_far.shape, so_far.dtype),
        scratch_shapes=fill_scratch(plan, count),
        input_output_aliases={2: 0},
        name="stored_table",
    )(bases, after, so_far)


def round_sizes(plan, stored):
    rounds = (plan.steps - stored) // PAIR
    batch = 1
    while batch * rounds < stored:
        batch *= 2
    return rounds, batch


def project_kernel(plan, stored, scale, devices):
    rounds, batch = round_sizes(plan, stored)
    depth = 2 * RANK * plan.examples
    parts = 4
    slab = plan.sub // parts

    def pick(grads, step):
        rank = step % RANK
        rows = lax.broadcasted_iota(jnp.int32, (RANK, plan.sub), 0) == rank
        parts = []
        for e in range(plan.examples):
            g = jnp.where(rows, grads[e, 0], 0.0)
            top = g.astype(jnp.bfloat16).astype(jnp.float32)
            parts += [top, g - top]
        return rows_of(parts).astype(jnp.bfloat16)

    def kernel(bases, grads, old_grads, tiles, out, acc, row_base, col_base):
        i = pl.program_id(0)

        @pl.when(i == 0)
        def _():
            acc[...] = jnp.zeros_like(acc)
            row_base[...] = row_offsets(plan)
            col_base[...] = column_keys(RANK)

        fix = 0.0
        olds, lefts, rows = [], [], []
        for q in range(batch):
            old = pick(old_grads, batch * i + q)
            old = jnp.where(batch * i + q < stored, old.astype(jnp.float32), 0.0)
            fix = fix + jnp.sum(old, axis=1, keepdims=True)
            olds.append((old * (1.0 / 65536.0)).astype(jnp.bfloat16))
        for p in range(PAIR):
            step = stored + PAIR * i + p
            rows.append(step_keys(step, bases, row_base[...]))
            left = pick(grads, step)
            fix = fix - 510.0 * jnp.sum(left.astype(jnp.float32), axis=1, keepdims=True)
            lefts.append([jnp.concatenate([left[:, b:b + slab]] * parts, axis=1) for b in range(0, plan.sub, slab)])
        for c in range(0, K, COLS):
            a = acc[:, c:c + COLS] + fix
            for p in range(PAIR):
                for n in range(parts):
                    planes = byte_planes(mixed(rows[p][n * slab:(n + 1) * slab], col_base[:, c:c + COLS]))
                    a = a + jnp.dot(lefts[p][n], rows_of(planes), preferred_element_type=jnp.float32)
            for q in range(batch):
                tile = jnp.concatenate([tiles[q, (c + n) // LANES] for n in range(0, COLS, LANES)], axis=1)
                a = a + jnp.dot(olds[q], tile, preferred_element_type=jnp.float32)
            acc[:, c:c + COLS] = a

        @pl.when(i == rounds - 1)
        def _():
            width = K // devices
            for e in range(plan.examples):
                part = acc[e * 2 * RANK:(e + 1) * 2 * RANK, :]
                total = jnp.sum(part, axis=0, keepdims=True) * scale
                for d in range(devices):
                    out[d, e:e + 1, :] = total[:, d * width:(d + 1) * width]

    return kernel, depth, rounds, batch


def project(plan, bases, grads, tiles, stored, scale, devices):
    kernel, depth, rounds, batch = project_kernel(plan, stored, scale, devices)
    smem = pl.BlockSpec(memory_space=pltpu.SMEM)
    parts = plan.block // plan.sub

    def place(step):
        number = step // RANK
        return (0, number // parts, 0, number % parts)

    last = stored // batch - 1
    return pl.pallas_call(
        kernel,
        grid=(rounds,),
        in_specs=[
            smem,
            pl.BlockSpec((plan.examples, 1, RANK, plan.sub), lambda i: place(PAIR * i + stored)),
            pl.BlockSpec((plan.examples, 1, RANK, plan.sub), lambda i: place(jnp.minimum(i, last) * batch)),
            pl.BlockSpec((batch, K // LANES, plan.sub, LANES), lambda i: (jnp.minimum(i, last), 0, 0, 0)),
        ],
        out_specs=pl.BlockSpec((devices, plan.examples, K // devices), lambda i: (0, 0, 0)),
        out_shape=jax.ShapeDtypeStruct((devices, plan.examples, K // devices), jnp.float32),
        scratch_shapes=[
            pltpu.VMEM((depth, K), jnp.float32),
            pltpu.VMEM((plan.sub, LANES), jnp.int32),
            pltpu.VMEM((RANK, K), jnp.int32),
        ],
        name="project",
    )(bases, grads, grads, tiles)


def swap(x, axis, bit):
    size = lax.axis_size(axis)
    return lax.ppermute(x, axis, [(i, i ^ (1 << bit)) for i in range(size)])


def shards(*args):
    data = args[:9]
    factors = args[9:14]
    mask, seeds = args[14:16]
    plan = Plan(tuple(x.shape[-1] for x in data), data[0].shape[0], lax.axis_size("proj"))
    table = jnp.asarray(plan.table)
    counts = [max(1, c * plan.steps // 128) for c in STORED_STEPS][:6]
    counts[-1] += -sum(counts) % PAIR
    starts = [sum(counts[:n]) for n in range(len(counts))]
    stored = sum(counts)
    own, tiles, bases = products(plan, data, factors, table, seeds, counts[0], stored)

    def cover(received, sent, number):
        nonlocal tiles
        tiles = stored_table(plan, bases, starts[number], counts[number], sent, tiles, number > 3)
        received, tiles = lax.optimization_barrier((received, tiles))
        return received

    if lax.axis_size("mp") == 2:
        other = swap(own, "mp", 0)
    else:
        own = lax.psum(own, "mp")
        other = jnp.zeros_like(own)
    other = cover(other, own, 1)
    other = pltpu.with_memory_space_constraint(other, pltpu.VMEM)
    keep, send, tiles = gradients(
        plan, data, own, other, mask.reshape(1, -1), plan.bits[0], bases, starts[2], counts[2], tiles)
    j = lax.axis_index("proj")
    low = len(plan.bits[:2])
    x = None
    for number, bit in enumerate(plan.bits[:2]):
        if number > 0:
            half = x.shape[0] // 2
            side = (j >> bit) & 1
            send = lax.dynamic_slice_in_dim(x, (1 - side) * half, half, 0)
            keep = lax.dynamic_slice_in_dim(x, side * half, half, 0)
        received = cover(swap(send, "proj", bit), send, number + 3)
        x = keep + received
    ways = plan.group >> low
    if ways > 1:
        size = x.shape[0] // ways
        place = (j >> low) % ways
        sends = [lax.dynamic_slice_in_dim(x, (place ^ d) * size, size, 0) for d in range(ways)]
        got = [lax.ppermute(sends[d], "proj", [(i, i ^ (d << low)) for i in range(plan.owners)]) for d in range(1, ways)]
        got = cover(got, sends[0], low + 3)
        x = sends[0]
        for one in got:
            x = x + one
    x = x[None]
    if plan.examples > 1:
        groups = [[e * plan.group + i for e in range(plan.examples)] for i in range(plan.group)]
        x = x.reshape((plan.examples, plan.own_blocks) + x.shape[2:])
        x = lax.all_to_all(x, "proj", 0, 0, axis_index_groups=groups, tiled=True)
    scale = 1.0 / (LENGTH * math.sqrt(21845.0 * K))
    devices = lax.axis_size("mp") * plan.owners
    pieces = project(plan, bases, x, tiles, stored, scale, devices)
    got = lax.all_to_all(pieces, ("mp", "proj"), 0, 0, tiled=True)
    return got.sum(axis=0)


def solution(mesh):
    in_specs = (
        P("proj", "mp"),
        P("proj", "mp"),
        P("proj", "mp"),
        P("proj", "mp"),
        P("proj", "mp"),
        P("proj", None, "mp"),
        P("proj", "mp"),
        P("proj", None, "mp"),
        P("proj", "mp"),
        P(None, None, "mp"),
        P(None, "mp"),
        P(None, None, "mp"),
        P(None, None, "mp"),
        P(None, None, "mp"),
        P("proj"),
        P(),
    )
    out_specs = P(None, ("mp", "proj"))
    return jax.shard_map(shards, mesh=mesh, in_specs=in_specs, out_specs=out_specs, check_vma=False)
```
